32 devices in a mesh: band: 4 (over z), lev: 4 (over y, core), grp: 2 (over x).
Axes of the slice: x: 2, y: 2, z: 4, core: 2. Of those that a mesh axis runs over, the one named last changes fastest.
Arguments:
- fourier: bfloat16 [3, 8, 2, 2, 2, 48, 96], P(None, 'lev', None, None, 'grp', 'band'), may hold values from -6 to 6
- legendre: bfloat16 [96, 2, 48, 2, 48], P('band', None, 'lev', 'grp'), may hold values from -0.625 to 0.625
- lat_points: int32 [2, 48], P('grp', 'band'), may hold values from 20 to 400, as said below
- wave_slots: int32 [96], replicated, may hold values from 0 to 95, as said below
- vertical: float32 [8, 8], replicated, may hold values from -2 to 2
Outputs:
- spectral: bfloat16 [96, 2, 4, 8, 2, 48], P('band', None, None, None, None, ('lev', 'grp'))
The draws below stay inside these ranges and needn't reach their ends.
Inputs may be any that keep to these rules, and one draw needn't show every extreme that they name: `lat_points`: the values are 20 + 4 i for i = 0 .. 95, each once (octahedral point counts of the latitude pairs, spread over devices). `wave_slots`: every wavenumber appears once; slots 2 i and 2 i + 1 hold wavenumbers m and 95 - m.
All inputs are finite; a program needn't handle non-finite values.
Results may differ from the reference program's by a relative error of at most 0.0053.
Values may be sent and summed in bfloat16 or wider, within the bound.
No kernel may reach another device: no remote copies, remote signals or barrier semaphores. Data moves between devices by JAX's collectives and lax.ppermute only.
A program may use at most 64 MiB of HBM per device.

```python
import jax
import jax.numpy as jnp
from jax import lax

M = 96
LEVELS = 8
FIELDS = 3
N_GRP = 2


def draw_lat_points(key, part):
    order = jax.random.permutation(jax.random.fold_in(key, 11), M).astype(jnp.int32)
    return (20 + 4 * order).astype(jnp.int32).reshape(N_GRP, M // N_GRP)


def draw_wave_slots(key, part):
    lower = jax.random.permutation(jax.random.fold_in(key, 23), M // 2).astype(jnp.int32)
    return jnp.stack([lower, M - 1 - lower], axis=1).reshape(M).astype(jnp.int32)


def raised(values, stream_key, source, target, shards_of, factor):
    owner, partner = [(jnp.arange(values.shape[position]) // (values.shape[position] // shards_of)).reshape([-1 if axis == position else 1 for axis in range(values.ndim)]) for position in (source, target)]
    chosen = jax.random.permutation(stream_key, shards_of)[partner]
    strong = (owner == chosen) | (owner == (partner + shards_of // 2) % shards_of)
    return jnp.where(strong, factor * values, values)


def level_of(rng, extent, split, low, largest):
    loudness = 1.0
    for dim, shards_of in split:
        draws = jax.random.uniform(jax.random.fold_in(jax.random.fold_in(rng, 6), dim), (shards_of,), jnp.float32, low / len(split), largest / len(split))
        loudness = loudness * jnp.repeat(jnp.exp(draws), extent[dim] // shards_of).reshape((-1,) + (1,) * (len(extent) - 1 - dim))
    return loudness


def bell_draw(stream_key, extent, scale, bound, split=(), held_as=jnp.bfloat16):
    drawn = jax.random.normal(stream_key, extent, jnp.float32) * scale
    if len(split) > 0:
        drawn = level_of(stream_key, extent, split, -0.22, 0.18) * drawn
    return jnp.clip(drawn, min=-bound, max=bound).astype(held_as)


def gaussian_with(key, dims, spread, reach, cuts, heavy, kind=jnp.bfloat16):
    result = spread * jax.random.normal(key, dims, jnp.float32)
    if cuts:
        result = result * level_of(key, dims, cuts, -0.22, 0.18)
    return jnp.clip(raised(result, jax.random.fold_in(key, 3), *heavy), -reach, reach).astype(kind)


def setup_inputs(seed: int = 0) -> dict:
    keys = jax.random.split(jax.random.key(seed), 6)
    fourier = bell_draw(keys[0], (FIELDS, LEVELS, 2, 2, N_GRP, M // N_GRP, M), 1.0, 6.0, ((1, 4), (4, 2), (5, 4)))
    legendre = gaussian_with(keys[1], (M, 2, M // 2, N_GRP, M // N_GRP), (2 * M) ** -0.5, 0.625, ((0, 4), (2, 4), (3, 2)), (3, 2, 2, 2.0))
    lat_points = draw_lat_points(jax.random.fold_in(keys[5], 71), 0)
    wave_slots = draw_wave_slots(jax.random.fold_in(keys[5], 71), 0)
    vertical = bell_draw(keys[4], (LEVELS, LEVELS), LEVELS ** -0.5, 2.0, (), jnp.float32)
    return {"fourier": fourier, "legendre": legendre, "lat_points": lat_points, "wave_slots": wave_slots, "vertical": vertical}


def per_slot(pieces):
    block, functions = pieces
    return jnp.einsum("cpr,pjr->pcj", block.astype(jnp.float32), functions.astype(jnp.float32), precision=lax.Precision.HIGHEST)


def reference(fourier, legendre, lat_points, wave_slots, vertical):
    cutoff = jnp.minimum(M - 1, (lat_points - 1) // 2)
    wave_ids = jnp.arange(M, dtype=jnp.int32)
    kept_mask = wave_ids[None, None, :] <= cutoff[:, :, None]
    masked = jnp.where(kept_mask, fourier, jnp.zeros((), fourier.dtype))
    ordered = jnp.take(masked, wave_slots, axis=6)
    level_ids = jnp.arange(LEVELS, dtype=jnp.int32)
    upper_part = level_ids[None, :] >= level_ids[:, None]
    integral = jnp.where(upper_part, vertical, jnp.zeros((), vertical.dtype))
    geopotential = jnp.einsum("lk,kcpgrs->lcpgrs", integral, ordered[2].astype(jnp.float32), precision=lax.Precision.HIGHEST).astype(jnp.bfloat16)
    fields = jnp.concatenate([ordered, geopotential[None]], axis=0)
    northern = fields[:, :, :, 0].astype(jnp.float32)
    southern = fields[:, :, :, 1].astype(jnp.float32)
    parity = jnp.stack([(northern + southern).astype(jnp.bfloat16), (northern - southern).astype(jnp.bfloat16)], axis=3)
    columns = parity.reshape((FIELDS + 1) * LEVELS * 2, 2, M, M)
    by_slot = jnp.transpose(columns, (3, 0, 1, 2))
    functions = legendre.reshape(M, 2, M // 2, M)
    raw = lax.map(per_slot, (by_slot, functions))
    raw = raw.reshape(M, 2, FIELDS + 1, LEVELS, 2, M // 2)
    half_ids = jnp.arange(M // 2, dtype=jnp.int32)
    parity_ids = jnp.arange(2, dtype=jnp.int32)
    total = wave_slots[:, None, None] + 2 * half_ids[None, None, :] + parity_ids[None, :, None]
    valid = (total <= M - 1)[:, :, None, None, None, :]
    return jnp.where(valid, raw, 0.0).astype(jnp.bfloat16)
```

```python
import jax
import jax.numpy as jnp
from jax import lax
from jax.sharding import PartitionSpec as P


def body(fourier, legendre, lat_points, wave_slots, vertical):
    wave_count = fourier.shape[6]
    cutoff = jnp.minimum(wave_count - 1, (lat_points - 1) // 2)
    wave_ids = lax.broadcasted_iota(jnp.int32, (1, 1, wave_count), 2)
    kept_mask = wave_ids <= cutoff[:, :, None]
    masked = jnp.where(kept_mask, fourier, jnp.zeros((), fourier.dtype))
    slot_table = (
        wave_slots[:, None] == lax.broadcasted_iota(jnp.int32, (wave_count, wave_count), 1)
    ).astype(jnp.bfloat16)
    ordered = lax.dot_general(
        slot_table, masked, (((1,), (6,)), ((), ())), preferred_element_type=jnp.float32
    ).astype(jnp.bfloat16)
    at_owners = lax.all_to_all(ordered, "band", split_axis=0, concat_axis=6, tiled=True)
    coeffs = lax.all_gather(at_owners, "lev", axis=2, tiled=True)
    level_count = coeffs.shape[2]
    level_rows = lax.broadcasted_iota(jnp.int32, (level_count, level_count), 0)
    level_cols = lax.broadcasted_iota(jnp.int32, (level_count, level_count), 1)
    integral = jnp.where(level_cols >= level_rows, vertical, jnp.zeros((), vertical.dtype))
    geopotential = jnp.einsum(
        "lk,skchgr->slchgr",
        integral,
        coeffs[:, 2].astype(jnp.float32),
        precision=lax.Precision.HIGHEST,
    ).astype(jnp.bfloat16)
    fields = jnp.concatenate([coeffs, geopotential[:, None]], axis=1)
    northern = fields[:, :, :, :, 0].astype(jnp.float32)
    southern = fields[:, :, :, :, 1].astype(jnp.float32)
    parity = jnp.stack(
        [(northern + southern).astype(jnp.bfloat16), (northern - southern).astype(jnp.bfloat16)],
        axis=4,
    )
    partial_value = lax.dot_general(
        parity, legendre, (((5, 6), (3, 4)), ((0, 4), (0, 1))), preferred_element_type=jnp.float32
    )
    groups = lax.axis_size("grp")
    half_count = partial_value.shape[5] // groups
    me = lax.axis_index("grp")
    summed = lax.dynamic_slice_in_dim(partial_value, me * half_count, half_count, 5)
    for step in range(1, groups):
        target = lax.rem(me + step, groups)
        piece = lax.dynamic_slice_in_dim(partial_value, target * half_count, half_count, 5)
        summed = summed + lax.ppermute(
            piece, "grp", [(i, (i + step) % groups) for i in range(groups)]
        )
    slot_count = summed.shape[0]
    slot_waves = lax.dynamic_slice_in_dim(
        wave_slots, lax.axis_index("band") * slot_count, slot_count
    )
    block_start = (lax.axis_index("lev") * groups + me) * half_count
    half_ids = block_start + lax.broadcasted_iota(jnp.int32, (1, 1, half_count), 2)
    parity_ids = lax.broadcasted_iota(jnp.int32, (1, 2, 1), 1)
    total = slot_waves[:, None, None] + 2 * half_ids + parity_ids
    valid = (total <= wave_count - 1)[:, :, None, None, None, :]
    return jnp.where(valid, summed, 0.0).astype(jnp.bfloat16)


def solution(mesh):
    placed = (
        P(None, "lev", None, None, "grp", "band", None),
        P("band", None, "lev", "grp", None),
        P("grp", "band"),
        P(),
        P(),
    )
    return jax.shard_map(
        body,
        mesh=mesh,
        in_specs=placed,
        out_specs=P("band", None, None, None, None, ("lev", "grp")),
        check_vma=False,
    )
```

```python
import functools

import jax
import jax.numpy as jnp
from jax import lax
from jax.experimental import pallas as pl
from jax.experimental.pallas import tpu as pltpu
from jax.sharding import PartitionSpec as P

F32, BF16 = jnp.float32, jnp.bfloat16
LANES = 128
GRANT = 8 << 20


def flipped(value, axis, step):
    return lax.ppermute(value, axis, [(i, i ^ step) for i in range(lax.axis_size(axis))])


def iota(shape, dim):
    return lax.broadcasted_iota(jnp.int32, shape, dim)


def prepare_kernel(dims, lat_ref, slots_ref, x_ref, slot_lanes_ref, *block_refs):
    fields, planes, pairs, slots, waves = dims
    width = LANES // planes
    band = lax.axis_index("band")
    x = x_ref[...].astype(F32)
    rows = x.shape[0]
    following = pltpu.roll(x, rows - 1, 0)
    previous = pltpu.roll(x, 1, 0)
    north = (iota(x.shape, 0) & 1) == 0
    parity = jnp.where(north, x + following, previous - x)
    pair_rows = iota((2 * pairs, waves), 0) // 2
    cutoff = jnp.zeros((2 * pairs, waves), jnp.int32)
    for q in range(pairs):
        cutoff = jnp.where(pair_rows == q, jnp.minimum(waves - 1, (lat_ref[0, q] - 1) // 2), cutoff)
    kept = iota((2 * pairs, waves), 1) <= cutoff
    parity = parity.reshape(fields * planes, 2 * pairs, waves)
    parity = jnp.where(kept[None], parity, 0.0)
    by_plane = jnp.concatenate(
        [parity[f * planes + plane] for plane in range(planes) for f in range(fields)], axis=0
    ).astype(BF16)
    lane = iota((8, LANES), 1)
    tables = []
    for k in range(len(block_refs)):
        first = (band ^ k) * slots
        held = jnp.full((8, LANES), -1, jnp.int32)
        for s in range(slots):
            held = jnp.where(lane % width == s, slots_ref[0, first + s], held)
        if k == 0:
            slot_lanes_ref[...] = held
        hot = iota((waves, LANES), 0) == held[0:1]
        tables.append(jnp.where(hot, 1.0, 0.0).astype(BF16))
    chosen = jnp.dot(by_plane, jnp.concatenate(tables, axis=1), preferred_element_type=F32)
    count = 2 * fields * pairs
    plane_of = iota((count, LANES), 1) // width
    for k, block_ref in enumerate(block_refs):
        mine = chosen[:, k * LANES : (k + 1) * LANES]
        block = mine[:count]
        for plane in range(1, planes):
            block = jnp.where(plane_of == plane, mine[plane * count : (plane + 1) * count], block)
        block_ref[...] = block.astype(BF16)


def spread_kernel(dims, own_ref, other_ref, out_ref, rows_ref):
    planes, slots, halves, sums = dims
    width = LANES // planes
    group = lax.axis_index("grp")
    block = iota((sums, LANES), 1) // width
    own = halves // 2
    for side, ref in enumerate((own_ref, other_ref)):
        rows_ref[side, :, :sums] = ref[...].astype(F32)
        for p in range(2):
            for first in range(0, halves, planes):
                pieces = []
                for part in range(planes):
                    start = (first + part) * 2 + p
                    pieces.append(rows_ref[side, pl.ds(start, slots, stride=2 * halves), :])
                    if width > slots:
                        pieces.append(jnp.zeros((width - slots, LANES), F32))
                turned = jnp.concatenate(pieces, axis=0).T[:sums]
                rolled = [turned] + [pltpu.roll(turned, d * width, 1) for d in range(1, planes)]
                for part in range(planes):
                    copies = rolled[-part % planes]
                    for plane in range(1, planes):
                        copies = jnp.where(block == plane, rolled[(plane - part) % planes], copies)
                    j = first + part
                    jj = j % own
                    if side == 0:
                        here, there = (jj // 2) * 8 + 6 + jj % 2, jj
                    else:
                        here, there = 8 + jj, 16 + jj
                    start = jnp.where(group == j // own, here, there)
                    out_ref[p, pl.ds(start, sums, stride=24), :] = copies


def sum_kernel(dims, *refs):
    fields, pairs, bands = dims
    blocks, (table_ref, total_ref, x_ref, y_ref, xy_ref, rows_ref) = refs[: 2 * bands], refs[2 * bands :]
    band = lax.axis_index("band")
    for i, block in enumerate(blocks):
        rows_ref[i] = block[...].astype(F32)
    for p in range(2):
        totals = [jnp.zeros((24, LANES), F32) for _ in range(2 * fields)]
        for k in range(bands):
            first = (band ^ k) * pairs
            for q in range(pairs):
                factors = table_ref[p, pl.ds(pl.multiple_of((first + q) * 24, 8), 24), :]
                for side in range(2):
                    for f in range(fields):
                        row = (f * pairs + q) * 2 + p
                        i = side * fields + f
                        totals[i] += rows_ref[side * bands + k, row : row + 1, :] * factors
        for i, total in enumerate(totals):
            total_ref[2 * i + p] = total
    for at, ref in ((0, x_ref), (8, y_ref), (16, xy_ref)):
        ref[...] = total_ref[:, at : at + 8, :].reshape(ref.shape).astype(BF16)


def finish_kernel(dims, vertical_ref, slot_lanes_ref, total_ref, x_ref, y_ref, xy_ref, out_ref, temps_ref, rows_ref):
    fields, levels, halves, slots, waves = dims
    planes = 2 * (levels // 4)
    width = LANES // planes
    lev, group = lax.axis_index("lev"), lax.axis_index("grp")
    y, core = lev // 2, lev % 2
    count = 4 * fields
    from_x, from_y, from_xy = (r[...].astype(F32).reshape(count, 8, LANES) for r in (x_ref, y_ref, xy_ref))
    half = (lev * 2 + group) * halves + iota((8, LANES), 0)
    valid = [slot_lanes_ref[...] + 2 * half + p <= waves - 1 for p in range(2)]

    def store(p, f, level, c, value):
        start = ((p * (fields + 1) + f) * levels + level) * (2 * halves) + c
        rows_ref[pl.ds(start, halves, stride=2), :] = value[:halves]

    for side in range(2):
        for f in range(fields):
            for p in range(2):
                n = (side * fields + f) * 2 + p
                kept = jnp.concatenate(
                    [total_ref[n, 6:8, :], total_ref[n, 14:16, :], total_ref[n, 22:24, :], jnp.zeros((2, LANES), F32)],
                    axis=0,
                )
                for far, value in enumerate((kept + from_x[n], from_y[n] + from_xy[n])):
                    value = jnp.where(valid[p], value, 0.0)
                    first = ((y ^ far) * 2 + (core ^ side)) * (levels // 4)
                    for plane in range(planes):
                        l, c = plane // 2, plane % 2
                        shifted = value if plane == 0 else pltpu.roll(value, LANES - plane * width, 1)
                        store(p, f, first + l, c, shifted)
                        if f == fields - 1:
                            temps_ref[first + l, 2 * p + c] = shifted
    for p in range(2):
        for c in range(2):
            temps = [temps_ref[k, 2 * p + c] for k in range(levels)]
            for level in range(levels):
                value = vertical_ref[level, level] * temps[level]
                for k in range(level + 1, levels):
                    value += vertical_ref[level, k] * temps[k]
                store(p, fields, level, c, value)
    out_ref[...] = rows_ref[:, :slots].astype(BF16)


SMEM = pl.BlockSpec(memory_space=pltpu.SMEM)
VMEM = pl.BlockSpec(memory_space=pltpu.VMEM)


def fast_body(fourier, legendre, lat_points, wave_slots, vertical):
    fields, local_levels, _, _, _, pairs, waves = fourier.shape
    slots, _, halves, _, sums = legendre.shape
    bands = lax.axis_size("band")
    levels = 4 * local_levels
    planes = 2 * local_levels
    shape = jax.ShapeDtypeStruct

    functions = legendre.transpose(0, 2, 3, 1, 4).reshape(slots * halves * 2, sums)
    other_functions = flipped(functions, "lev", 2)

    rows = fourier.transpose(0, 1, 2, 4, 5, 3, 6).reshape(-1, waves)
    block = shape((2 * fields * pairs, LANES), BF16)
    slot_lanes, *blocks = pl.pallas_call(
        functools.partial(prepare_kernel, (fields, planes, pairs, slots, waves)),
        in_specs=[SMEM, SMEM, VMEM],
        out_specs=[VMEM] * (1 + bands),
        out_shape=[shape((8, LANES), jnp.int32)] + [block] * bands,
        compiler_params=pltpu.CompilerParams(vmem_limit_bytes=GRANT),
        name="prepare",
    )(lat_points, wave_slots.reshape(1, -1), rows)

    own = {0: blocks[0]}
    for k in reversed(range(1, bands)):
        own[k] = flipped(blocks[k], "band", k)
    table = pl.pallas_call(
        functools.partial(spread_kernel, (planes, slots, halves, sums)),
        in_specs=[VMEM] * 2,
        out_specs=VMEM,
        out_shape=shape((2, sums * 24, LANES), F32),
        scratch_shapes=[pltpu.VMEM((2, slots * halves * 2, LANES), F32)],
        compiler_params=pltpu.CompilerParams(vmem_limit_bytes=GRANT),
        name="spread",
    )(functions, other_functions)
    other = {k: flipped(own[k], "lev", 1) for k in (0, *reversed(range(1, bands)))}

    count = 4 * fields
    message = shape((count * 8, LANES), BF16)
    total, to_x, to_y, to_xy = pl.pallas_call(
        functools.partial(sum_kernel, (fields, pairs, bands)),
        in_specs=[VMEM] * (2 * bands + 1),
        out_specs=[VMEM] * 4,
        out_shape=[shape((count, 24, LANES), F32)] + [message] * 3,
        scratch_shapes=[pltpu.VMEM((2 * bands, *block.shape), F32)],
        compiler_params=pltpu.CompilerParams(vmem_limit_bytes=GRANT),
        name="sum",
    )(*[own[k] for k in range(bands)], *[other[k] for k in range(bands)], table)

    lev_grp = [(i, i ^ 5) for i in range(8)]
    from_xy = lax.ppermute(to_xy, ("lev", "grp"), lev_grp)
    from_x = flipped(to_x, "grp", 1)
    from_y = flipped(to_y, "lev", 2)
    own_halves = halves // 2
    out_rows = 2 * (fields + 1) * levels * own_halves * 2
    out = pl.pallas_call(
        functools.partial(finish_kernel, (fields, levels, own_halves, slots, waves)),
        in_specs=[SMEM] + [VMEM] * 5,
        out_specs=VMEM,
        out_shape=shape((out_rows, slots), BF16),
        scratch_shapes=[pltpu.VMEM((levels, 4, 8, LANES), F32), pltpu.VMEM((out_rows, LANES), F32)],
        compiler_params=pltpu.CompilerParams(vmem_limit_bytes=GRANT),
        name="finish",
    )(vertical, slot_lanes, total, from_x, from_y, from_xy)
    out = out.reshape(2, fields + 1, levels, own_halves, 2, slots)
    return out.transpose(5, 0, 1, 2, 4, 3)


def fits(mesh, fourier, legendre):
    bands, levs, groups = (mesh.shape[a] for a in ("band", "lev", "grp"))
    fields, levels, _, _, _, pairs, waves = fourier.shape
    slots, _, halves, _, sums = legendre.shape
    planes = 2 * levels // levs
    return (
        levs == 4
        and groups == 2
        and bands & (bands - 1) == 0
        and waves <= LANES
        and sums <= LANES
        and halves // levs == 12
        and LANES % planes == 0
        and 12 % planes == 0
        and slots // bands <= LANES // planes
        and slots // bands % 8 == 0
        and 2 * pairs // bands % 8 == 0
        and sums % 8 == 0
    )


def general_body(fourier, legendre, lat_points, wave_slots, vertical):
    wave_count = fourier.shape[6]
    cutoff = jnp.minimum(wave_count - 1, (lat_points - 1) // 2)
    wave_ids = lax.broadcasted_iota(jnp.int32, (1, 1, wave_count), 2)
    kept_mask = wave_ids <= cutoff[:, :, None]
    masked = jnp.where(kept_mask, fourier, jnp.zeros((), fourier.dtype))
    slot_table = (
        wave_slots[:, None] == lax.broadcasted_iota(jnp.int32, (wave_count, wave_count), 1)
    ).astype(jnp.bfloat16)
    ordered = lax.dot_general(
        slot_table, masked, (((1,), (6,)), ((), ())), preferred_element_type=jnp.float32
    ).astype(jnp.bfloat16)
    at_owners = lax.all_to_all(ordered, "band", split_axis=0, concat_axis=6, tiled=True)
    coeffs = lax.all_gather(at_owners, "lev", axis=2, tiled=True)
    level_count = coeffs.shape[2]
    level_rows = lax.broadcasted_iota(jnp.int32, (level_count, level_count), 0)
    level_cols = lax.broadcasted_iota(jnp.int32, (level_count, level_count), 1)
    integral = jnp.where(level_cols >= level_rows, vertical, jnp.zeros((), vertical.dtype))
    geopotential = jnp.einsum(
        "lk,skchgr->slchgr",
        integral,
        coeffs[:, 2].astype(jnp.float32),
        precision=lax.Precision.HIGHEST,
    ).astype(jnp.bfloat16)
    fields = jnp.concatenate([coeffs, geopotential[:, None]], axis=1)
    northern = fields[:, :, :, :, 0].astype(jnp.float32)
    southern = fields[:, :, :, :, 1].astype(jnp.float32)
    parity = jnp.stack(
        [(northern + southern).astype(jnp.bfloat16), (northern - southern).astype(jnp.bfloat16)],
        axis=4,
    )
    partial_value = lax.dot_general(
        parity, legendre, (((5, 6), (3, 4)), ((0, 4), (0, 1))), preferred_element_type=jnp.float32
    )
    groups = lax.axis_size("grp")
    half_count = partial_value.shape[5] // groups
    me = lax.axis_index("grp")
    summed = lax.dynamic_slice_in_dim(partial_value, me * half_count, half_count, 5)
    for step in range(1, groups):
        target = lax.rem(me + step, groups)
        piece = lax.dynamic_slice_in_dim(partial_value, target * half_count, half_count, 5)
        summed = summed + lax.ppermute(
            piece, "grp", [(i, (i + step) % groups) for i in range(groups)]
        )
    slot_count = summed.shape[0]
    slot_waves = lax.dynamic_slice_in_dim(
        wave_slots, lax.axis_index("band") * slot_count, slot_count
    )
    block_start = (lax.axis_index("lev") * groups + me) * half_count
    half_ids = block_start + lax.broadcasted_iota(jnp.int32, (1, 1, half_count), 2)
    parity_ids = lax.broadcasted_iota(jnp.int32, (1, 2, 1), 1)
    total = slot_waves[:, None, None] + 2 * half_ids + parity_ids
    valid = (total <= wave_count - 1)[:, :, None, None, None, :]
    return jnp.where(valid, summed, 0.0).astype(jnp.bfloat16)


def solution(mesh):
    def program(fourier, legendre, lat_points, wave_slots, vertical):
        placed = (
            P(None, "lev", None, None, "grp", "band", None),
            P("band", None, "lev", "grp", None),
            P("grp", "band"),
            P(),
            P(),
        )
        step = jax.shard_map(
            fast_body if fits(mesh, fourier, legendre) else general_body,
            mesh=mesh,
            in_specs=placed,
            out_specs=P("band", None, None, None, None, ("lev", "grp")),
            check_vma=False,
        )
        return step(fourier, legendre, lat_points, wave_slots, vertical)

    return program
```

```python
import functools

import jax
import jax.numpy as jnp
from jax import lax
from jax.experimental import pallas as pl
from jax.experimental.pallas import tpu as pltpu
from jax.sharding import PartitionSpec as P

F32, BF16 = jnp.float32, jnp.bfloat16
LANES = 128
GRANT = 8 << 20


def flipped(value, axis, step):
    return lax.ppermute(value, axis, [(i, i ^ step) for i in range(lax.axis_size(axis))])


def iota(shape, dim):
    return lax.broadcasted_iota(jnp.int32, shape, dim)


def prepare_kernel(dims, lat_hbm, slots_hbm, x_hbm, functions_hbm, vertical_hbm, slot_lanes_ref, functions_ref, vertical_ref, *rest):
    fields, planes, pairs, slots, waves = dims
    block_refs, (lat_ref, slots_ref, x_ref, sems) = rest[:-4], rest[-4:]
    width = LANES // planes
    band = lax.axis_index("band")
    copies = [
        pltpu.make_async_copy(source, target, sems.at[i])
        for i, (source, target) in enumerate(
            (
                (slots_hbm, slots_ref),
                (lat_hbm, lat_ref),
                (x_hbm, x_ref),
                (functions_hbm, functions_ref),
                (vertical_hbm, vertical_ref),
            )
        )
    ]
    for copy in copies:
        copy.start()
    lane = iota((8, LANES), 1)
    copies[0].wait()
    tables = []
    for k in range(len(block_refs)):
        first = (band ^ k) * slots
        held = jnp.full((8, LANES), -1, jnp.int32)
        for s in range(slots):
            held = jnp.where(lane % width == s, slots_ref[0, first + s], held)
        if k == 0:
            slot_lanes_ref[...] = held
        hot = iota((waves, LANES), 0) == held[0:1]
        tables.append(jnp.where(hot, 1.0, 0.0).astype(BF16))
    pair_rows = iota((2 * pairs, waves), 0) // 2
    cutoff = jnp.zeros((2 * pairs, waves), jnp.int32)
    copies[1].wait()
    for q in range(pairs):
        cutoff = jnp.where(pair_rows == q, jnp.minimum(waves - 1, (lat_ref[0, q] - 1) // 2), cutoff)
    kept = iota((2 * pairs, waves), 1) <= cutoff
    copies[2].wait()
    x = x_ref[...].astype(F32)
    rows = x.shape[0]
    following = pltpu.roll(x, rows - 1, 0)
    previous = pltpu.roll(x, 1, 0)
    north = (iota(x.shape, 0) & 1) == 0
    parity = jnp.where(north, x + following, previous - x)
    parity = parity.reshape(fields * planes, 2 * pairs, waves)
    parity = jnp.where(kept[None], parity, 0.0)
    by_plane = jnp.concatenate(
        [parity[f * planes + plane] for plane in range(planes) for f in range(fields)], axis=0
    ).astype(BF16)
    chosen = jnp.dot(by_plane, jnp.concatenate(tables, axis=1), preferred_element_type=F32)
    count = 2 * fields * pairs
    plane_of = iota((count, LANES), 1) // width
    for k, block_ref in enumerate(block_refs):
        mine = chosen[:, k * LANES : (k + 1) * LANES]
        block = mine[:count]
        for plane in range(1, planes):
            block = jnp.where(plane_of == plane, mine[plane * count : (plane + 1) * count], block)
        block_ref[...] = block.astype(BF16)
    copies[3].wait()
    copies[4].wait()


def spread_kernel(dims, own_ref, other_ref, vertical_ref, out_ref, weights_ref, rows_ref):
    planes, slots, halves, sums = dims
    width = LANES // planes
    group = lax.axis_index("grp")
    block = iota((sums, LANES), 1) // width
    own = halves // 2
    levels = vertical_ref.shape[0]
    for level in range(levels):
        for k in range(level, levels):
            weights_ref[level * levels + k] = jnp.broadcast_to(vertical_ref[level : level + 1, k : k + 1], (8, LANES))
    for side, ref in enumerate((own_ref, other_ref)):
        rows_ref[side, :, :sums] = ref[...].astype(F32)
        for p in range(2):
            for first in range(0, halves, planes):
                pieces = []
                for part in range(planes):
                    start = (first + part) * 2 + p
                    pieces.append(rows_ref[side, pl.ds(start, slots, stride=2 * halves), :])
                    if width > slots:
                        pieces.append(jnp.zeros((width - slots, LANES), F32))
                turned = jnp.concatenate(pieces, axis=0).T[:sums]
                rolled = [turned] + [pltpu.roll(turned, d * width, 1) for d in range(1, planes)]
                for part in range(planes):
                    copies = rolled[-part % planes]
                    for plane in range(1, planes):
                        copies = jnp.where(block == plane, rolled[(plane - part) % planes], copies)
                    j = first + part
                    jj = j % own
                    if side == 0:
                        here, there = (jj // 2) * 8 + 6 + jj % 2, jj
                    else:
                        here, there = 8 + jj, 16 + jj
                    start = jnp.where(group == j // own, here, there)
                    out_ref[p, pl.ds(start, sums, stride=24), :] = copies


def sum_kernel(dims, *refs):
    fields, pairs, bands = dims
    blocks, (table_ref, total_ref, x_ref, y_ref, xy_ref, rows_ref) = refs[: 2 * bands], refs[2 * bands :]
    band = lax.axis_index("band")
    for i, block in enumerate(blocks):
        rows_ref[i] = block[...].astype(F32)
    for p in range(2):
        totals = [jnp.zeros((24, LANES), F32) for _ in range(2 * fields)]
        for k in range(bands):
            first = (band ^ k) * pairs
            for q in range(pairs):
                factors = table_ref[p, pl.ds(pl.multiple_of((first + q) * 24, 8), 24), :]
                for side in range(2):
                    for f in range(fields):
                        row = (f * pairs + q) * 2 + p
                        i = side * fields + f
                        totals[i] += rows_ref[side * bands + k, row : row + 1, :] * factors
        for i, total in enumerate(totals):
            total_ref[2 * i + p] = total
    for at, ref in ((0, x_ref), (8, y_ref), (16, xy_ref)):
        ref[...] = total_ref[:, at : at + 8, :].reshape(ref.shape).astype(BF16)


def finish_kernel(dims, weights_ref, slot_lanes_ref, total_ref, x_ref, y_ref, xy_ref, out_ref, temps_ref, rows_ref):
    fields, levels, halves, slots, waves = dims
    planes = 2 * (levels // 4)
    width = LANES // planes
    lev, group = lax.axis_index("lev"), lax.axis_index("grp")
    y, core = lev // 2, lev % 2
    count = 4 * fields
    from_x, from_y, from_xy = (r[...].astype(F32).reshape(count, 8, LANES) for r in (x_ref, y_ref, xy_ref))
    half = (lev * 2 + group) * halves + iota((8, LANES), 0)
    valid = [slot_lanes_ref[...] + 2 * half + p <= waves - 1 for p in range(2)]

    def store(p, f, level, c, value):
        start = ((p * (fields + 1) + f) * levels + level) * (2 * halves) + c
        rows_ref[pl.ds(start, halves, stride=2), :] = value[:halves]

    for side in range(2):
        for f in range(fields):
            for p in range(2):
                n = (side * fields + f) * 2 + p
                kept = jnp.concatenate(
                    [total_ref[n, 6:8, :], total_ref[n, 14:16, :], total_ref[n, 22:24, :], jnp.zeros((2, LANES), F32)],
                    axis=0,
                )
                for far, value in enumerate((kept + from_x[n], from_y[n] + from_xy[n])):
                    value = jnp.where(valid[p], value, 0.0)
                    first = ((y ^ far) * 2 + (core ^ side)) * (levels // 4)
                    for plane in range(planes):
                        l, c = plane // 2, plane % 2
                        shifted = value if plane == 0 else pltpu.roll(value, LANES - plane * width, 1)
                        store(p, f, first + l, c, shifted)
                        if f == fields - 1:
                            temps_ref[first + l, 2 * p + c] = shifted
    for p in range(2):
        for c in range(2):
            temps = [temps_ref[k, 2 * p + c] for k in range(levels)]
            for level in range(levels):
                value = weights_ref[level * levels + level] * temps[level]
                for k in range(level + 1, levels):
                    value += weights_ref[level * levels + k] * temps[k]
                store(p, fields, level, c, value)
    out_ref[...] = rows_ref[:, :slots].astype(BF16)


HBM = pl.BlockSpec(memory_space=pltpu.HBM)
VMEM = pl.BlockSpec(memory_space=pltpu.VMEM)


def fast_body(fourier, legendre, lat_points, wave_slots, vertical):
    fields, local_levels, _, _, _, pairs, waves = fourier.shape
    slots, _, halves, _, sums = legendre.shape
    bands = lax.axis_size("band")
    levels = 4 * local_levels
    planes = 2 * local_levels
    shape = jax.ShapeDtypeStruct

    functions = legendre.transpose(0, 2, 3, 1, 4).reshape(slots * halves * 2, sums)
    other_functions = flipped(functions, "lev", 2)

    rows = fourier.transpose(0, 1, 2, 4, 5, 3, 6).reshape(-1, waves)
    block = shape((2 * fields * pairs, LANES), BF16)
    slot_lanes, functions, vertical, *blocks = pl.pallas_call(
        functools.partial(prepare_kernel, (fields, planes, pairs, slots, waves)),
        in_specs=[HBM] * 5,
        out_specs=[VMEM] * (3 + bands),
        out_shape=[
            shape((8, LANES), jnp.int32),
            shape(functions.shape, BF16),
            shape(vertical.shape, F32),
        ]
        + [block] * bands,
        scratch_shapes=[
            pltpu.SMEM(lat_points.shape, jnp.int32),
            pltpu.SMEM((1, wave_slots.size), jnp.int32),
            pltpu.VMEM(rows.shape, BF16),
            pltpu.SemaphoreType.DMA((5,)),
        ],
        compiler_params=pltpu.CompilerParams(vmem_limit_bytes=GRANT),
        name="prepare",
    )(*[pltpu.with_memory_space_constraint(v, pltpu.HBM) for v in (lat_points, wave_slots.reshape(1, -1), rows, functions, vertical)])

    far = tuple(reversed(range(1, bands)))
    own = {0: blocks[0]}
    for k in far:
        own[k] = flipped(blocks[k], "band", k)
    table, weights = pl.pallas_call(
        functools.partial(spread_kernel, (planes, slots, halves, sums)),
        in_specs=[VMEM] * 3,
        out_specs=[VMEM] * 2,
        out_shape=[shape((2, sums * 24, LANES), F32), shape((levels * levels, 8, LANES), F32)],
        scratch_shapes=[pltpu.VMEM((2, slots * halves * 2, LANES), F32)],
        compiler_params=pltpu.CompilerParams(vmem_limit_bytes=GRANT),
        name="spread",
    )(functions, other_functions, vertical)
    other = {}
    for k in (0, *far):
        other[k] = flipped(own[k], "lev", 1)

    count = 4 * fields
    message = shape((count * 8, LANES), BF16)
    total, to_x, to_y, to_xy = pl.pallas_call(
        functools.partial(sum_kernel, (fields, pairs, bands)),
        in_specs=[VMEM] * (2 * bands + 1),
        out_specs=[VMEM] * 4,
        out_shape=[shape((count, 24, LANES), F32)] + [message] * 3,
        scratch_shapes=[pltpu.VMEM((2 * bands, *block.shape), F32)],
        compiler_params=pltpu.CompilerParams(vmem_limit_bytes=GRANT),
        name="sum",
    )(*[own[k] for k in range(bands)], *[other[k] for k in range(bands)], table)

    from_xy = lax.ppermute(to_xy, ("lev", "grp"), [(i, i ^ 5) for i in range(8)])
    from_x = flipped(to_x, "grp", 1)
    from_y = flipped(to_y, "lev", 2)
    own_halves = halves // 2
    out_rows = 2 * (fields + 1) * levels * own_halves * 2
    out = pl.pallas_call(
        functools.partial(finish_kernel, (fields, levels, own_halves, slots, waves)),
        in_specs=[VMEM] * 6,
        out_specs=VMEM,
        out_shape=shape((out_rows, slots), BF16),
        scratch_shapes=[pltpu.VMEM((levels, 4, 8, LANES), F32), pltpu.VMEM((out_rows, LANES), F32)],
        compiler_params=pltpu.CompilerParams(vmem_limit_bytes=GRANT),
        name="finish",
    )(weights, slot_lanes, total, from_x, from_y, from_xy)
    out = out.reshape(2, fields + 1, levels, own_halves, 2, slots)
    return out.transpose(5, 0, 1, 2, 4, 3)


def fits(mesh, fourier, legendre):
    bands, levs, groups = (mesh.shape[a] for a in ("band", "lev", "grp"))
    _, levels, _, _, _, pairs, waves = fourier.shape
    slots, _, halves, _, sums = legendre.shape
    planes = 2 * levels // levs
    return (
        levs == 4
        and groups == 2
        and bands & (bands - 1) == 0
        and waves <= LANES
        and sums <= LANES
        and halves // levs == 12
        and LANES % planes == 0
        and 12 % planes == 0
        and slots // bands <= LANES // planes
        and slots // bands % 8 == 0
        and 2 * pairs // bands % 8 == 0
        and sums % 8 == 0
    )


def general_body(fourier, legendre, lat_points, wave_slots, vertical):
    wave_count = fourier.shape[6]
    cutoff = jnp.minimum(wave_count - 1, (lat_points - 1) // 2)
    wave_ids = lax.broadcasted_iota(jnp.int32, (1, 1, wave_count), 2)
    kept_mask = wave_ids <= cutoff[:, :, None]
    masked = jnp.where(kept_mask, fourier, jnp.zeros((), fourier.dtype))
    slot_table = (
        wave_slots[:, None] == lax.broadcasted_iota(jnp.int32, (wave_count, wave_count), 1)
    ).astype(jnp.bfloat16)
    ordered = lax.dot_general(
        slot_table, masked, (((1,), (6,)), ((), ())), preferred_element_type=jnp.float32
    ).astype(jnp.bfloat16)
    at_owners = lax.all_to_all(ordered, "band", split_axis=0, concat_axis=6, tiled=True)
    coeffs = lax.all_gather(at_owners, "lev", axis=2, tiled=True)
    level_count = coeffs.shape[2]
    level_rows = lax.broadcasted_iota(jnp.int32, (level_count, level_count), 0)
    level_cols = lax.broadcasted_iota(jnp.int32, (level_count, level_count), 1)
    integral = jnp.where(level_cols >= level_rows, vertical, jnp.zeros((), vertical.dtype))
    geopotential = jnp.einsum(
        "lk,skchgr->slchgr",
        integral,
        coeffs[:, 2].astype(jnp.float32),
        precision=lax.Precision.HIGHEST,
    ).astype(jnp.bfloat16)
    fields = jnp.concatenate([coeffs, geopotential[:, None]], axis=1)
    northern = fields[:, :, :, :, 0].astype(jnp.float32)
    southern = fields[:, :, :, :, 1].astype(jnp.float32)
    parity = jnp.stack(
        [(northern + southern).astype(jnp.bfloat16), (northern - southern).astype(jnp.bfloat16)],
        axis=4,
    )
    partial_value = lax.dot_general(
        parity, legendre, (((5, 6), (3, 4)), ((0, 4), (0, 1))), preferred_element_type=jnp.float32
    )
    groups = lax.axis_size("grp")
    half_count = partial_value.shape[5] // groups
    me = lax.axis_index("grp")
    summed = lax.dynamic_slice_in_dim(partial_value, me * half_count, half_count, 5)
    for step in range(1, groups):
        target = lax.rem(me + step, groups)
        piece = lax.dynamic_slice_in_dim(partial_value, target * half_count, half_count, 5)
        summed = summed + lax.ppermute(
            piece, "grp", [(i, (i + step) % groups) for i in range(groups)]
        )
    slot_count = summed.shape[0]
    slot_waves = lax.dynamic_slice_in_dim(
        wave_slots, lax.axis_index("band") * slot_count, slot_count
    )
    block_start = (lax.axis_index("lev") * groups + me) * half_count
    half_ids = block_start + lax.broadcasted_iota(jnp.int32, (1, 1, half_count), 2)
    parity_ids = lax.broadcasted_iota(jnp.int32, (1, 2, 1), 1)
    total = slot_waves[:, None, None] + 2 * half_ids + parity_ids
    valid = (total <= wave_count - 1)[:, :, None, None, None, :]
    return jnp.where(valid, summed, 0.0).astype(jnp.bfloat16)


def solution(mesh):
    def program(fourier, legendre, lat_points, wave_slots, vertical):
        placed = (
            P(None, "lev", None, None, "grp", "band", None),
            P("band", None, "lev", "grp", None),
            P("grp", "band"),
            P(),
            P(),
        )
        fast = fits(mesh, fourier, legendre)
        step = jax.shard_map(
            fast_body if fast else general_body,
            mesh=mesh,
            in_specs=placed,
            out_specs=P("band", None, None, None, None, ("lev", "grp")),
            check_vma=False,
        )
        return step(fourier, legendre, lat_points, wave_slots, vertical)

    return program
```

```python
import functools

import jax
import jax.numpy as jnp
from jax import lax
from jax.experimental import pallas as pl
from jax.experimental.pallas import tpu as pltpu
from jax.sharding import PartitionSpec as P

F32, BF16 = jnp.float32, jnp.bfloat16
LANES = 128
GRANT = 8 << 20


def flipped(value, axis, step):
    return lax.ppermute(value, axis, [(i, i ^ step) for i in range(lax.axis_size(axis))])


def crossed(step):
    bands, levs = lax.axis_size("band"), lax.axis_size("lev")
    return [(b * levs + v, (b + step) % bands * levs + (v ^ 1)) for b in range(bands) for v in range(levs)]


def iota(shape, dim):
    return lax.broadcasted_iota(jnp.int32, shape, dim)


def prepare_kernel(dims, lat_hbm, slots_hbm, x_hbm, functions_hbm, vertical_hbm, slot_lanes_ref, functions_ref, vertical_ref, *rest):
    fields, planes, pairs, slots, waves = dims
    block_refs, (lat_ref, slots_ref, x_ref, sems) = rest[:-4], rest[-4:]
    width = LANES // planes
    band = lax.axis_index("band")
    copies = [
        pltpu.make_async_copy(source, target, sems.at[i])
        for i, (source, target) in enumerate(
            (
                (slots_hbm, slots_ref),
                (lat_hbm, lat_ref),
                (x_hbm, x_ref),
                (functions_hbm, functions_ref),
                (vertical_hbm, vertical_ref),
            )
        )
    ]
    for copy in copies:
        copy.start()
    lane = iota((8, LANES), 1)
    copies[0].wait()
    tables = []
    for k in range(len(block_refs)):
        first = lax.rem(band + k, len(block_refs)) * slots
        held = jnp.full((8, LANES), -1, jnp.int32)
        for s in range(slots):
            held = jnp.where(lane % width == s, slots_ref[0, first + s], held)
        if k == 0:
            slot_lanes_ref[...] = held
        hot = iota((waves, LANES), 0) == held[0:1]
        tables.append(jnp.where(hot, 1.0, 0.0).astype(BF16))
    pair_rows = iota((2 * pairs, waves), 0) // 2
    cutoff = jnp.zeros((2 * pairs, waves), jnp.int32)
    copies[1].wait()
    for q in range(pairs):
        cutoff = jnp.where(pair_rows == q, jnp.minimum(waves - 1, (lat_ref[0, q] - 1) // 2), cutoff)
    kept = iota((2 * pairs, waves), 1) <= cutoff
    copies[2].wait()
    x = x_ref[...].astype(F32)
    rows = x.shape[0]
    following = pltpu.roll(x, rows - 1, 0)
    previous = pltpu.roll(x, 1, 0)
    north = (iota(x.shape, 0) & 1) == 0
    parity = jnp.where(north, x + following, previous - x)
    parity = parity.reshape(fields * planes, 2 * pairs, waves)
    parity = jnp.where(kept[None], parity, 0.0)
    by_plane = jnp.concatenate(
        [parity[f * planes + plane] for plane in range(planes) for f in range(fields)], axis=0
    ).astype(BF16)
    chosen = jnp.dot(by_plane, jnp.concatenate(tables, axis=1), preferred_element_type=F32)
    count = 2 * fields * pairs
    plane_of = iota((count, LANES), 1) // width
    for k, block_ref in enumerate(block_refs):
        mine = chosen[:, k * LANES : (k + 1) * LANES]
        block = mine[:count]
        for plane in range(1, planes):
            block = jnp.where(plane_of == plane, mine[plane * count : (plane + 1) * count], block)
        block_ref[...] = block.astype(BF16)
    copies[3].wait()
    copies[4].wait()


def spread_kernel(dims, own_ref, other_ref, vertical_ref, out_ref, weights_ref, rows_ref):
    planes, slots, halves, sums = dims
    width = LANES // planes
    group = lax.axis_index("grp")
    block = iota((sums, LANES), 1) // width
    own = halves // 2
    levels = vertical_ref.shape[0]
    for level in range(levels):
        for k in range(level, levels):
            weights_ref[level * levels + k] = jnp.broadcast_to(vertical_ref[level : level + 1, k : k + 1], (8, LANES))
    for side, ref in enumerate((own_ref, other_ref)):
        rows_ref[side, :, :sums] = ref[...].astype(F32)
        for p in range(2):
            for first in range(0, halves, planes):
                pieces = []
                for part in range(planes):
                    start = (first + part) * 2 + p
                    pieces.append(rows_ref[side, pl.ds(start, slots, stride=2 * halves), :])
                    if width > slots:
                        pieces.append(jnp.zeros((width - slots, LANES), F32))
                turned = jnp.concatenate(pieces, axis=0).T[:sums]
                rolled = [turned] + [pltpu.roll(turned, d * width, 1) for d in range(1, planes)]
                for part in range(planes):
                    copies = rolled[-part % planes]
                    for plane in range(1, planes):
                        copies = jnp.where(block == plane, rolled[(plane - part) % planes], copies)
                    j = first + part
                    jj = j % own
                    if side == 0:
                        here, there = (jj // 2) * 8 + 6 + jj % 2, jj
                    else:
                        here, there = 8 + jj, 16 + jj
                    start = jnp.where(group == j // own, here, there)
                    out_ref[p, pl.ds(start, sums, stride=24), :] = copies


def sum_kernel(dims, *refs):
    fields, pairs, bands = dims
    blocks, (table_ref, total_ref, x_ref, y_ref, xy_ref, rows_ref) = refs[: 2 * bands], refs[2 * bands :]
    band = lax.axis_index("band")
    for i, block in enumerate(blocks):
        rows_ref[i] = block[...].astype(F32)
    for p in range(2):
        totals = [jnp.zeros((24, LANES), F32) for _ in range(2 * fields)]
        for k in range(bands):
            first = lax.rem(band + bands - k, bands) * pairs
            for q in range(pairs):
                factors = table_ref[p, pl.ds(pl.multiple_of((first + q) * 24, 8), 24), :]
                for side in range(2):
                    for f in range(fields):
                        row = (f * pairs + q) * 2 + p
                        i = side * fields + f
                        totals[i] += rows_ref[side * bands + k, row : row + 1, :] * factors
        for i, total in enumerate(totals):
            total_ref[2 * i + p] = total
    for at, ref in ((0, x_ref), (8, y_ref), (16, xy_ref)):
        ref[...] = total_ref[:, at : at + 8, :].reshape(ref.shape).astype(BF16)


def finish_kernel(dims, weights_ref, slot_lanes_ref, total_ref, x_ref, y_ref, xy_ref, out_ref, temps_ref, rows_ref):
    fields, levels, halves, slots, waves = dims
    planes = 2 * (levels // 4)
    width = LANES // planes
    lev, group = lax.axis_index("lev"), lax.axis_index("grp")
    y, core = lev // 2, lev % 2
    count = 4 * fields
    from_x, from_y, from_xy = (r[...].astype(F32).reshape(count, 8, LANES) for r in (x_ref, y_ref, xy_ref))
    half = (lev * 2 + group) * halves + iota((8, LANES), 0)
    valid = [slot_lanes_ref[...] + 2 * half + p <= waves - 1 for p in range(2)]

    def store(p, f, level, c, value):
        start = ((p * (fields + 1) + f) * levels + level) * (2 * halves) + c
        rows_ref[pl.ds(start, halves, stride=2), :] = value[:halves]

    for side in range(2):
        for f in range(fields):
            for p in range(2):
                n = (side * fields + f) * 2 + p
                far_n = ((1 - side) * fields + f) * 2 + p
                kept = jnp.concatenate(
                    [total_ref[n, 6:8, :], total_ref[n, 14:16, :], total_ref[n, 22:24, :], jnp.zeros((2, LANES), F32)],
                    axis=0,
                )
                for far, value in enumerate((kept + from_x[n], from_y[far_n] + from_xy[far_n])):
                    value = jnp.where(valid[p], value, 0.0)
                    first = ((y ^ far) * 2 + (core ^ side)) * (levels // 4)
                    for plane in range(planes):
                        l, c = plane // 2, plane % 2
                        shifted = value if plane == 0 else pltpu.roll(value, LANES - plane * width, 1)
                        store(p, f, first + l, c, shifted)
                        if f == fields - 1:
                            temps_ref[first + l, 2 * p + c] = shifted
    for p in range(2):
        for c in range(2):
            temps = [temps_ref[k, 2 * p + c] for k in range(levels)]
            for level in range(levels):
                value = weights_ref[level * levels + level] * temps[level]
                for k in range(level + 1, levels):
                    value += weights_ref[level * levels + k] * temps[k]
                store(p, fields, level, c, value)
    out_ref[...] = rows_ref[:, :slots].astype(BF16)


HBM = pl.BlockSpec(memory_space=pltpu.HBM)
VMEM = pl.BlockSpec(memory_space=pltpu.VMEM)


def fast_body(fourier, legendre, lat_points, wave_slots, vertical):
    fields, local_levels, _, _, _, pairs, waves = fourier.shape
    slots, _, halves, _, sums = legendre.shape
    bands = lax.axis_size("band")
    levels = 4 * local_levels
    planes = 2 * local_levels
    shape = jax.ShapeDtypeStruct

    functions = legendre.transpose(0, 2, 3, 1, 4).reshape(slots * halves * 2, sums)
    other_functions = flipped(functions, "lev", 3)

    rows = fourier.transpose(0, 1, 2, 4, 5, 3, 6).reshape(-1, waves)
    block = shape((2 * fields * pairs, LANES), BF16)
    slot_lanes, functions, vertical, *blocks = pl.pallas_call(
        functools.partial(prepare_kernel, (fields, planes, pairs, slots, waves)),
        in_specs=[HBM] * 5,
        out_specs=[VMEM] * (3 + bands),
        out_shape=[
            shape((8, LANES), jnp.int32),
            shape(functions.shape, BF16),
            shape(vertical.shape, F32),
        ]
        + [block] * bands,
        scratch_shapes=[
            pltpu.SMEM(lat_points.shape, jnp.int32),
            pltpu.SMEM((1, wave_slots.size), jnp.int32),
            pltpu.VMEM(rows.shape, BF16),
            pltpu.SemaphoreType.DMA((5,)),
        ],
        compiler_params=pltpu.CompilerParams(vmem_limit_bytes=GRANT),
        name="prepare",
    )(*[pltpu.with_memory_space_constraint(v, pltpu.HBM) for v in (lat_points, wave_slots.reshape(1, -1), rows, functions, vertical)])

    steps = tuple(range(1, bands))
    own = {0: blocks[0]}
    for k in steps:
        own[k] = lax.ppermute(blocks[k], ("band", "lev"), crossed(k))
    table, weights = pl.pallas_call(
        functools.partial(spread_kernel, (planes, slots, halves, sums)),
        in_specs=[VMEM] * 3,
        out_specs=[VMEM] * 2,
        out_shape=[shape((2, sums * 24, LANES), F32), shape((levels * levels, 8, LANES), F32)],
        scratch_shapes=[pltpu.VMEM((2, slots * halves * 2, LANES), F32)],
        compiler_params=pltpu.CompilerParams(vmem_limit_bytes=GRANT),
        name="spread",
    )(functions, other_functions, vertical)
    other = {}
    for k in (0, *steps):
        other[k] = flipped(own[k], "lev", 1)

    count = 4 * fields
    message = shape((count * 8, LANES), BF16)
    total, to_x, to_y, to_xy = pl.pallas_call(
        functools.partial(sum_kernel, (fields, pairs, bands)),
        in_specs=[VMEM] * (2 * bands + 1),
        out_specs=[VMEM] * 4,
        out_shape=[shape((count, 24, LANES), F32)] + [message] * 3,
        scratch_shapes=[pltpu.VMEM((2 * bands, *block.shape), F32)],
        compiler_params=pltpu.CompilerParams(vmem_limit_bytes=GRANT),
        name="sum",
    )(own[0], *[other[k] for k in steps], other[0], *[own[k] for k in steps], table)

    from_xy = lax.ppermute(to_xy, ("lev", "grp"), [(i, i ^ 7) for i in range(8)])
    from_x = flipped(to_x, "grp", 1)
    from_y = flipped(to_y, "lev", 3)
    own_halves = halves // 2
    out_rows = 2 * (fields + 1) * levels * own_halves * 2
    out = pl.pallas_call(
        functools.partial(finish_kernel, (fields, levels, own_halves, slots, waves)),
        in_specs=[VMEM] * 6,
        out_specs=VMEM,
        out_shape=shape((out_rows, slots), BF16),
        scratch_shapes=[pltpu.VMEM((levels, 4, 8, LANES), F32), pltpu.VMEM((out_rows, LANES), F32)],
        compiler_params=pltpu.CompilerParams(vmem_limit_bytes=GRANT),
        name="finish",
    )(weights, slot_lanes, total, from_x, from_y, from_xy)
    out = out.reshape(2, fields + 1, levels, own_halves, 2, slots)
    return out.transpose(5, 0, 1, 2, 4, 3)


def fits(mesh, fourier, legendre):
    bands, levs, groups = (mesh.shape[a] for a in ("band", "lev", "grp"))
    _, levels, _, _, _, pairs, waves = fourier.shape
    slots, _, halves, _, sums = legendre.shape
    planes = 2 * levels // levs
    return (
        levs == 4
        and groups == 2
        and bands & (bands - 1) == 0
        and waves <= LANES
        and sums <= LANES
        and halves // levs == 12
        and LANES % planes == 0
        and 12 % planes == 0
        and slots // bands <= LANES // planes
        and slots // bands % 8 == 0
        and 2 * pairs // bands % 8 == 0
        and sums % 8 == 0
    )


def general_body(fourier, legendre, lat_points, wave_slots, vertical):
    wave_count = fourier.shape[6]
    cutoff = jnp.minimum(wave_count - 1, (lat_points - 1) // 2)
    wave_ids = lax.broadcasted_iota(jnp.int32, (1, 1, wave_count), 2)
    kept_mask = wave_ids <= cutoff[:, :, None]
    masked = jnp.where(kept_mask, fourier, jnp.zeros((), fourier.dtype))
    slot_table = (
        wave_slots[:, None] == lax.broadcasted_iota(jnp.int32, (wave_count, wave_count), 1)
    ).astype(jnp.bfloat16)
    ordered = lax.dot_general(
        slot_table, masked, (((1,), (6,)), ((), ())), preferred_element_type=jnp.float32
    ).astype(jnp.bfloat16)
    at_owners = lax.all_to_all(ordered, "band", split_axis=0, concat_axis=6, tiled=True)
    coeffs = lax.all_gather(at_owners, "lev", axis=2, tiled=True)
    level_count = coeffs.shape[2]
    level_rows = lax.broadcasted_iota(jnp.int32, (level_count, level_count), 0)
    level_cols = lax.broadcasted_iota(jnp.int32, (level_count, level_count), 1)
    integral = jnp.where(level_cols >= level_rows, vertical, jnp.zeros((), vertical.dtype))
    geopotential = jnp.einsum(
        "lk,skchgr->slchgr",
        integral,
        coeffs[:, 2].astype(jnp.float32),
        precision=lax.Precision.HIGHEST,
    ).astype(jnp.bfloat16)
    fields = jnp.concatenate([coeffs, geopotential[:, None]], axis=1)
    northern = fields[:, :, :, :, 0].astype(jnp.float32)
    southern = fields[:, :, :, :, 1].astype(jnp.float32)
    parity = jnp.stack(
        [(northern + southern).astype(jnp.bfloat16), (northern - southern).astype(jnp.bfloat16)],
        axis=4,
    )
    partial_value = lax.dot_general(
        parity, legendre, (((5, 6), (3, 4)), ((0, 4), (0, 1))), preferred_element_type=jnp.float32
    )
    groups = lax.axis_size("grp")
    half_count = partial_value.shape[5] // groups
    me = lax.axis_index("grp")
    summed = lax.dynamic_slice_in_dim(partial_value, me * half_count, half_count, 5)
    for step in range(1, groups):
        target = lax.rem(me + step, groups)
        piece = lax.dynamic_slice_in_dim(partial_value, target * half_count, half_count, 5)
        summed = summed + lax.ppermute(
            piece, "grp", [(i, (i + step) % groups) for i in range(groups)]
        )
    slot_count = summed.shape[0]
    slot_waves = lax.dynamic_slice_in_dim(
        wave_slots, lax.axis_index("band") * slot_count, slot_count
    )
    block_start = (lax.axis_index("lev") * groups + me) * half_count
    half_ids = block_start + lax.broadcasted_iota(jnp.int32, (1, 1, half_count), 2)
    parity_ids = lax.broadcasted_iota(jnp.int32, (1, 2, 1), 1)
    total = slot_waves[:, None, None] + 2 * half_ids + parity_ids
    valid = (total <= wave_count - 1)[:, :, None, None, None, :]
    return jnp.where(valid, summed, 0.0).astype(jnp.bfloat16)


def solution(mesh):
    def program(fourier, legendre, lat_points, wave_slots, vertical):
        placed = (
            P(None, "lev", None, None, "grp", "band", None),
            P("band", None, "lev", "grp", None),
            P("grp", "band"),
            P(),
            P(),
        )
        fast = fits(mesh, fourier, legendre)
        step = jax.shard_map(
            fast_body if fast else general_body,
            mesh=mesh,
            in_specs=placed,
            out_specs=P("band", None, None, None, None, ("lev", "grp")),
            check_vma=False,
        )
        return step(fourier, legendre, lat_points, wave_slots, vertical)

    return program
```

```python
import functools

import jax
import jax.numpy as jnp
from jax import lax
from jax.experimental import pallas as pl
from jax.experimental.pallas import tpu as pltpu
from jax.sharding import PartitionSpec as P

F32, BF16 = jnp.float32, jnp.bfloat16
LANES = 128
GRANT = 8 << 20


def flipped(value, axis, step):
    return lax.ppermute(value, axis, [(i, i ^ step) for i in range(lax.axis_size(axis))])


def rounds(bands):
    if bands == 4:
        return ((2, 3, 1, 0), (3, 2, 0, 1), (1, 0, 3, 2))
    return tuple(tuple((b + k) % bands for b in range(bands)) for k in range(1, bands))


def picked(table, index):
    value = jnp.int32(table[0])
    for i in range(1, len(table)):
        value = jnp.where(index == i, table[i], value)
    return value


def target(bands, band, k):
    return picked(rounds(bands)[k - 1], band) if k else band


def source(bands, band, k):
    return picked([rounds(bands)[k - 1].index(b) for b in range(bands)], band) if k else band


def crossed(k):
    bands, levs = lax.axis_size("band"), lax.axis_size("lev")
    to = rounds(bands)[k - 1]
    return [(b * levs + v, to[b] * levs + (v ^ 1)) for b in range(bands) for v in range(levs)]


def iota(shape, dim):
    return lax.broadcasted_iota(jnp.int32, shape, dim)


def prepare_kernel(dims, lat_hbm, slots_hbm, x_hbm, functions_hbm, vertical_hbm, slot_lanes_ref, functions_ref, vertical_ref, *rest):
    fields, planes, pairs, slots, waves = dims
    block_refs, (lat_ref, slots_ref, x_ref, sems) = rest[:-4], rest[-4:]
    width = LANES // planes
    band = lax.axis_index("band")
    copies = [
        pltpu.make_async_copy(given, held, sems.at[i])
        for i, (given, held) in enumerate(
            (
                (slots_hbm, slots_ref),
                (lat_hbm, lat_ref),
                (x_hbm, x_ref),
                (functions_hbm, functions_ref),
                (vertical_hbm, vertical_ref),
            )
        )
    ]
    for copy in copies:
        copy.start()
    lane = iota((8, LANES), 1)
    copies[0].wait()
    tables = []
    for k in range(len(block_refs)):
        first = target(len(block_refs), band, k) * slots
        held = jnp.full((8, LANES), -1, jnp.int32)
        for s in range(slots):
            held = jnp.where(lane % width == s, slots_ref[0, first + s], held)
        if k == 0:
            slot_lanes_ref[...] = held
        hot = iota((waves, LANES), 0) == held[0:1]
        tables.append(jnp.where(hot, 1.0, 0.0).astype(BF16))
    pair_rows = iota((2 * pairs, waves), 0) // 2
    cutoff = jnp.zeros((2 * pairs, waves), jnp.int32)
    copies[1].wait()
    for q in range(pairs):
        cutoff = jnp.where(pair_rows == q, jnp.minimum(waves - 1, (lat_ref[0, q] - 1) // 2), cutoff)
    kept = iota((2 * pairs, waves), 1) <= cutoff
    copies[2].wait()
    x = x_ref[...].astype(F32)
    rows = x.shape[0]
    following = pltpu.roll(x, rows - 1, 0)
    previous = pltpu.roll(x, 1, 0)
    north = (iota(x.shape, 0) & 1) == 0
    parity = jnp.where(north, x + following, previous - x)
    parity = parity.reshape(fields * planes, 2 * pairs, waves)
    parity = jnp.where(kept[None], parity, 0.0)
    by_plane = jnp.concatenate(
        [parity[f * planes + plane] for plane in range(planes) for f in range(fields)], axis=0
    ).astype(BF16)
    chosen = jnp.dot(by_plane, jnp.concatenate(tables, axis=1), preferred_element_type=F32)
    count = 2 * fields * pairs
    plane_of = iota((count, LANES), 1) // width
    for k, block_ref in enumerate(block_refs):
        mine = chosen[:, k * LANES : (k + 1) * LANES]
        block = mine[:count]
        for plane in range(1, planes):
            block = jnp.where(plane_of == plane, mine[plane * count : (plane + 1) * count], block)
        block_ref[...] = block.astype(BF16)
    copies[3].wait()
    copies[4].wait()


def spread_kernel(dims, own_ref, other_ref, vertical_ref, out_ref, weights_ref, rows_ref):
    planes, slots, halves, sums = dims
    width = LANES // planes
    group = lax.axis_index("grp")
    block = iota((sums, LANES), 1) // width
    own = halves // 2
    levels = vertical_ref.shape[0]
    for level in range(levels):
        for k in range(level, levels):
            weights_ref[level * levels + k] = jnp.broadcast_to(vertical_ref[level : level + 1, k : k + 1], (8, LANES))
    for side, ref in enumerate((own_ref, other_ref)):
        rows_ref[side, :, :sums] = ref[...].astype(F32)
        for p in range(2):
            for first in range(0, halves, planes):
                pieces = []
                for part in range(planes):
                    start = (first + part) * 2 + p
                    pieces.append(rows_ref[side, pl.ds(start, slots, stride=2 * halves), :])
                    if width > slots:
                        pieces.append(jnp.zeros((width - slots, LANES), F32))
                turned = jnp.concatenate(pieces, axis=0).T[:sums]
                rolled = [turned] + [pltpu.roll(turned, d * width, 1) for d in range(1, planes)]
                for part in range(planes):
                    copies = rolled[-part % planes]
                    for plane in range(1, planes):
                        copies = jnp.where(block == plane, rolled[(plane - part) % planes], copies)
                    j = first + part
                    jj = j % own
                    if side == 0:
                        here, there = (jj // 2) * 8 + 6 + jj % 2, jj
                    else:
                        here, there = 8 + jj, 16 + jj
                    start = jnp.where(group == j // own, here, there)
                    out_ref[p, pl.ds(start, sums, stride=24), :] = copies


def add_products(dims, parts, table_ref, rows_ref, p, totals):
    fields, pairs, bands = dims
    band = lax.axis_index("band")
    for i, (side, k) in enumerate(parts):
        first = source(bands, band, k) * pairs
        for q in range(pairs):
            factors = table_ref[p, pl.ds(pl.multiple_of((first + q) * 24, 8), 24), :]
            for f in range(fields):
                row = (f * pairs + q) * 2 + p
                totals[side * fields + f] += rows_ref[i, row : row + 1, :] * factors


def sum_first_kernel(dims, parts, *refs):
    block_refs, (table_ref, total_ref, rows_ref) = refs[:-3], refs[-3:]
    for i, block_ref in enumerate(block_refs):
        rows_ref[i] = block_ref[...].astype(F32)
    for p in range(2):
        totals = [jnp.zeros((24, LANES), F32) for _ in range(2 * dims[0])]
        add_products(dims, parts, table_ref, rows_ref, p, totals)
        for i, total in enumerate(totals):
            total_ref[2 * i + p] = total


def sum_kernel(dims, parts, *refs):
    block_refs, (table_ref, before_ref, total_ref, x_ref, y_ref, xy_ref, rows_ref) = refs[:-7], refs[-7:]
    for i, block_ref in enumerate(block_refs):
        rows_ref[i] = block_ref[...].astype(F32)
    for p in range(2):
        totals = [before_ref[2 * i + p] for i in range(2 * dims[0])]
        add_products(dims, parts, table_ref, rows_ref, p, totals)
        for i, total in enumerate(totals):
            total_ref[2 * i + p] = total
    for at, ref in ((0, x_ref), (8, y_ref), (16, xy_ref)):
        ref[...] = total_ref[:, at : at + 8, :].reshape(ref.shape).astype(BF16)


def finish_kernel(dims, weights_ref, slot_lanes_ref, total_ref, x_ref, y_ref, xy_ref, out_ref, temps_ref, rows_ref):
    fields, levels, halves, slots, waves = dims
    planes = 2 * (levels // 4)
    width = LANES // planes
    lev, group = lax.axis_index("lev"), lax.axis_index("grp")
    y, core = lev // 2, lev % 2
    count = 4 * fields
    from_x, from_y, from_xy = (r[...].astype(F32).reshape(count, 8, LANES) for r in (x_ref, y_ref, xy_ref))
    half = (lev * 2 + group) * halves + iota((8, LANES), 0)
    valid = [slot_lanes_ref[...] + 2 * half + p <= waves - 1 for p in range(2)]

    def store(p, f, level, c, value):
        start = ((p * (fields + 1) + f) * levels + level) * (2 * halves) + c
        rows_ref[pl.ds(start, halves, stride=2), :] = value[:halves]

    for side in range(2):
        for f in range(fields):
            for p in range(2):
                n = (side * fields + f) * 2 + p
                far_n = ((1 - side) * fields + f) * 2 + p
                kept = jnp.concatenate(
                    [total_ref[n, 6:8, :], total_ref[n, 14:16, :], total_ref[n, 22:24, :], jnp.zeros((2, LANES), F32)],
                    axis=0,
                )
                for far, value in enumerate((kept + from_x[n], from_y[far_n] + from_xy[far_n])):
                    value = jnp.where(valid[p], value, 0.0)
                    first = ((y ^ far) * 2 + (core ^ side)) * (levels // 4)
                    for plane in range(planes):
                        l, c = plane // 2, plane % 2
                        shifted = value if plane == 0 else pltpu.roll(value, LANES - plane * width, 1)
                        store(p, f, first + l, c, shifted)
                        if f == fields - 1:
                            temps_ref[first + l, 2 * p + c] = shifted
    for p in range(2):
        for c in range(2):
            temps = [temps_ref[k, 2 * p + c] for k in range(levels)]
            for level in range(levels):
                value = weights_ref[level * levels + level] * temps[level]
                for k in range(level + 1, levels):
                    value += weights_ref[level * levels + k] * temps[k]
                store(p, fields, level, c, value)
    out_ref[...] = rows_ref[:, :slots].astype(BF16)


HBM = pl.BlockSpec(memory_space=pltpu.HBM)
VMEM = pl.BlockSpec(memory_space=pltpu.VMEM)


def fast_body(fourier, legendre, lat_points, wave_slots, vertical):
    fields, local_levels, _, _, _, pairs, waves = fourier.shape
    slots, _, halves, _, sums = legendre.shape
    bands = lax.axis_size("band")
    levels = 4 * local_levels
    planes = 2 * local_levels
    shape = jax.ShapeDtypeStruct

    functions = legendre.transpose(0, 2, 3, 1, 4).reshape(slots * halves * 2, sums)
    other_functions = flipped(functions, "lev", 3)

    rows = fourier.transpose(0, 1, 2, 4, 5, 3, 6).reshape(-1, waves)
    block = shape((2 * fields * pairs, LANES), BF16)
    slot_lanes, functions, vertical, *blocks = pl.pallas_call(
        functools.partial(prepare_kernel, (fields, planes, pairs, slots, waves)),
        in_specs=[HBM] * 5,
        out_specs=[VMEM] * (3 + bands),
        out_shape=[
            shape((8, LANES), jnp.int32),
            shape(functions.shape, BF16),
            shape(vertical.shape, F32),
        ]
        + [block] * bands,
        scratch_shapes=[
            pltpu.SMEM(lat_points.shape, jnp.int32),
            pltpu.SMEM((1, wave_slots.size), jnp.int32),
            pltpu.VMEM(rows.shape, BF16),
            pltpu.SemaphoreType.DMA((5,)),
        ],
        compiler_params=pltpu.CompilerParams(vmem_limit_bytes=GRANT),
        name="prepare",
    )(*[pltpu.with_memory_space_constraint(v, pltpu.HBM) for v in (lat_points, wave_slots.reshape(1, -1), rows, functions, vertical)])

    steps = tuple(range(1, bands))
    own = {0: blocks[0]}
    for k in steps:
        own[k] = lax.ppermute(blocks[k], ("band", "lev"), crossed(k))
    table, weights = pl.pallas_call(
        functools.partial(spread_kernel, (planes, slots, halves, sums)),
        in_specs=[VMEM] * 3,
        out_specs=[VMEM] * 2,
        out_shape=[shape((2, sums * 24, LANES), F32), shape((levels * levels, 8, LANES), F32)],
        scratch_shapes=[pltpu.VMEM((2, slots * halves * 2, LANES), F32)],
        compiler_params=pltpu.CompilerParams(vmem_limit_bytes=GRANT),
        name="spread",
    )(functions, other_functions, vertical)
    other = {}
    for k in (0, *steps):
        other[k] = flipped(own[k], "lev", 1)

    count = 4 * fields
    message = shape((count * 8, LANES), BF16)
    totals = shape((count, 24, LANES), F32)
    direct = [(0, 0), *[(1, k) for k in steps]]
    before = pl.pallas_call(
        functools.partial(sum_first_kernel, (fields, pairs, bands), direct),
        in_specs=[VMEM] * (bands + 1),
        out_specs=VMEM,
        out_shape=totals,
        scratch_shapes=[pltpu.VMEM((bands, *block.shape), F32)],
        compiler_params=pltpu.CompilerParams(vmem_limit_bytes=GRANT),
        name="sum_first",
    )(*[own[k] for k in range(bands)], table)
    total, to_x, to_y, to_xy = pl.pallas_call(
        functools.partial(sum_kernel, (fields, pairs, bands), [(1 - side, k) for side, k in direct]),
        in_specs=[VMEM] * (bands + 2),
        out_specs=[VMEM] * 4,
        out_shape=[totals] + [message] * 3,
        scratch_shapes=[pltpu.VMEM((bands, *block.shape), F32)],
        compiler_params=pltpu.CompilerParams(vmem_limit_bytes=GRANT),
        name="sum",
    )(*[other[k] for k in range(bands)], table, before)

    from_xy = lax.ppermute(to_xy, ("lev", "grp"), [(i, i ^ 7) for i in range(8)])
    from_x = flipped(to_x, "grp", 1)
    from_y = flipped(to_y, "lev", 3)
    own_halves = halves // 2
    out_rows = 2 * (fields + 1) * levels * own_halves * 2
    out = pl.pallas_call(
        functools.partial(finish_kernel, (fields, levels, own_halves, slots, waves)),
        in_specs=[VMEM] * 6,
        out_specs=VMEM,
        out_shape=shape((out_rows, slots), BF16),
        scratch_shapes=[pltpu.VMEM((levels, 4, 8, LANES), F32), pltpu.VMEM((out_rows, LANES), F32)],
        compiler_params=pltpu.CompilerParams(vmem_limit_bytes=GRANT),
        name="finish",
    )(weights, slot_lanes, total, from_x, from_y, from_xy)
    out = out.reshape(2, fields + 1, levels, own_halves, 2, slots)
    return out.transpose(5, 0, 1, 2, 4, 3)


def fits(mesh, fourier, legendre):
    bands, levs, groups = (mesh.shape[a] for a in ("band", "lev", "grp"))
    _, levels, _, _, _, pairs, waves = fourier.shape
    slots, _, halves, _, sums = legendre.shape
    planes = 2 * levels // levs
    return (
        levs == 4
        and groups == 2
        and bands & (bands - 1) == 0
        and waves <= LANES
        and sums <= LANES
        and halves // levs == 12
        and LANES % planes == 0
        and 12 % planes == 0
        and slots // bands <= LANES // planes
        and slots // bands % 8 == 0
        and 2 * pairs // bands % 8 == 0
        and sums % 8 == 0
    )


def general_body(fourier, legendre, lat_points, wave_slots, vertical):
    wave_count = fourier.shape[6]
    cutoff = jnp.minimum(wave_count - 1, (lat_points - 1) // 2)
    wave_ids = lax.broadcasted_iota(jnp.int32, (1, 1, wave_count), 2)
    kept_mask = wave_ids <= cutoff[:, :, None]
    masked = jnp.where(kept_mask, fourier, jnp.zeros((), fourier.dtype))
    slot_table = (
        wave_slots[:, None] == lax.broadcasted_iota(jnp.int32, (wave_count, wave_count), 1)
    ).astype(jnp.bfloat16)
    ordered = lax.dot_general(
        slot_table, masked, (((1,), (6,)), ((), ())), preferred_element_type=jnp.float32
    ).astype(jnp.bfloat16)
    at_owners = lax.all_to_all(ordered, "band", split_axis=0, concat_axis=6, tiled=True)
    coeffs = lax.all_gather(at_owners, "lev", axis=2, tiled=True)
    level_count = coeffs.shape[2]
    level_rows = lax.broadcasted_iota(jnp.int32, (level_count, level_count), 0)
    level_cols = lax.broadcasted_iota(jnp.int32, (level_count, level_count), 1)
    integral = jnp.where(level_cols >= level_rows, vertical, jnp.zeros((), vertical.dtype))
    geopotential = jnp.einsum(
        "lk,skchgr->slchgr",
        integral,
        coeffs[:, 2].astype(jnp.float32),
        precision=lax.Precision.HIGHEST,
    ).astype(jnp.bfloat16)
    fields = jnp.concatenate([coeffs, geopotential[:, None]], axis=1)
    northern = fields[:, :, :, :, 0].astype(jnp.float32)
    southern = fields[:, :, :, :, 1].astype(jnp.float32)
    parity = jnp.stack(
        [(northern + southern).astype(jnp.bfloat16), (northern - southern).astype(jnp.bfloat16)],
        axis=4,
    )
    partial_value = lax.dot_general(
        parity, legendre, (((5, 6), (3, 4)), ((0, 4), (0, 1))), preferred_element_type=jnp.float32
    )
    groups = lax.axis_size("grp")
    half_count = partial_value.shape[5] // groups
    me = lax.axis_index("grp")
    summed = lax.dynamic_slice_in_dim(partial_value, me * half_count, half_count, 5)
    for step in range(1, groups):
        target = lax.rem(me + step, groups)
        piece = lax.dynamic_slice_in_dim(partial_value, target * half_count, half_count, 5)
        summed = summed + lax.ppermute(
            piece, "grp", [(i, (i + step) % groups) for i in range(groups)]
        )
    slot_count = summed.shape[0]
    slot_waves = lax.dynamic_slice_in_dim(
        wave_slots, lax.axis_index("band") * slot_count, slot_count
    )
    block_start = (lax.axis_index("lev") * groups + me) * half_count
    half_ids = block_start + lax.broadcasted_iota(jnp.int32, (1, 1, half_count), 2)
    parity_ids = lax.broadcasted_iota(jnp.int32, (1, 2, 1), 1)
    total = slot_waves[:, None, None] + 2 * half_ids + parity_ids
    valid = (total <= wave_count - 1)[:, :, None, None, None, :]
    return jnp.where(valid, summed, 0.0).astype(jnp.bfloat16)


def solution(mesh):
    def program(fourier, legendre, lat_points, wave_slots, vertical):
        placed = (
            P(None, "lev", None, None, "grp", "band", None),
            P("band", None, "lev", "grp", None),
            P("grp", "band"),
            P(),
            P(),
        )
        fast = fits(mesh, fourier, legendre)
        step = jax.shard_map(
            fast_body if fast else general_body,
            mesh=mesh,
            in_specs=placed,
            out_specs=P("band", None, None, None, None, ("lev", "grp")),
            check_vma=False,
        )
        return step(fourier, legendre, lat_points, wave_slots, vertical)

    return program
```

```python
import functools

import jax
import jax.numpy as jnp
from jax import lax
from jax.experimental import pallas as pl
from jax.experimental.pallas import tpu as pltpu
from jax.sharding import PartitionSpec as P

F32, BF16 = jnp.float32, jnp.bfloat16
LANES = 128
GRANT = 8 << 20
PIECES = 3


def flipped(value, axis, step):
    return lax.ppermute(value, axis, [(i, i ^ step) for i in range(lax.axis_size(axis))])


def rounds(bands):
    if bands == 4:
        return ((2, 3, 1, 0), (3, 2, 0, 1), (1, 0, 3, 2))
    return tuple(tuple((b + k) % bands for b in range(bands)) for k in range(1, bands))


def picked(table, index):
    value = jnp.int32(table[0])
    for i in range(1, len(table)):
        value = jnp.where(index == i, table[i], value)
    return value


def target(bands, band, k):
    return picked(rounds(bands)[k - 1], band) if k else band


def source(bands, band, k):
    return picked([rounds(bands)[k - 1].index(b) for b in range(bands)], band) if k else band


def crossed(k):
    bands, levs = lax.axis_size("band"), lax.axis_size("lev")
    to = rounds(bands)[k - 1]
    return [(b * levs + v, to[b] * levs + (v ^ 1)) for b in range(bands) for v in range(levs)]


def iota(shape, dim):
    return lax.broadcasted_iota(jnp.int32, shape, dim)


def prepare_kernel(dims, lat_hbm, slots_hbm, x_hbm, functions_hbm, vertical_hbm, slot_lanes_ref, functions_ref, vertical_ref, *rest):
    fields, planes, pairs, slots, waves = dims
    block_refs, (lat_ref, slots_ref, x_ref, sems) = rest[:-4], rest[-4:]
    width = LANES // planes
    band = lax.axis_index("band")
    share = x_ref.shape[0] // PIECES
    pieces = [pl.ds(i * share, share) for i in range(PIECES)]
    copies = [
        pltpu.make_async_copy(given, held, sems.at[i])
        for i, (given, held) in enumerate(
            (
                (slots_hbm, slots_ref),
                (lat_hbm, lat_ref),
                *((x_hbm.at[piece], x_ref.at[piece]) for piece in pieces),
                (functions_hbm, functions_ref),
                (vertical_hbm, vertical_ref),
            )
        )
    ]
    for copy in copies:
        copy.start()
    lane = iota((8, LANES), 1)
    copies[0].wait()
    tables = []
    for k in range(len(block_refs)):
        first = target(len(block_refs), band, k) * slots
        held = jnp.full((8, LANES), -1, jnp.int32)
        for s in range(slots):
            held = jnp.where(lane % width == s, slots_ref[0, first + s], held)
        if k == 0:
            slot_lanes_ref[...] = held
        hot = iota((waves, LANES), 0) == held[0:1]
        tables.append(jnp.where(hot, 1.0, 0.0).astype(BF16))
    pair_rows = iota((2 * pairs, waves), 0) >> 1
    points = jnp.zeros((2 * pairs, waves), jnp.int32)
    copies[1].wait()
    for q in range(pairs):
        points = jnp.where(pair_rows == q, lat_ref[0, q], points)
    cutoff = jnp.minimum(waves - 1, (points - 1) >> 1)
    kept = iota((2 * pairs, waves), 1) <= cutoff
    for copy in copies[2 : 2 + PIECES]:
        copy.wait()
    x = x_ref[...].astype(F32)
    rows = x.shape[0]
    following = pltpu.roll(x, rows - 1, 0)
    previous = pltpu.roll(x, 1, 0)
    north = (iota(x.shape, 0) & 1) == 0
    parity = jnp.where(north, x + following, previous - x)
    parity = parity.reshape(fields * planes, 2 * pairs, waves)
    parity = jnp.where(kept[None], parity, 0.0)
    by_plane = jnp.concatenate(
        [parity[f * planes + plane] for plane in range(planes) for f in range(fields)], axis=0
    ).astype(BF16)
    chosen = jnp.dot(by_plane, jnp.concatenate(tables, axis=1), preferred_element_type=F32)
    count = 2 * fields * pairs
    plane_of = iota((count, LANES), 1) // width
    for k, block_ref in enumerate(block_refs):
        mine = chosen[:, k * LANES : (k + 1) * LANES]
        block = mine[:count]
        for plane in range(1, planes):
            block = jnp.where(plane_of == plane, mine[plane * count : (plane + 1) * count], block)
        block_ref[...] = block.astype(BF16)
    for copy in copies[2 + PIECES :]:
        copy.wait()


def spread_kernel(dims, own_ref, other_ref, vertical_ref, out_ref, weights_ref, rows_ref):
    planes, slots, halves, sums = dims
    width = LANES // planes
    group = lax.axis_index("grp")
    block = iota((sums, LANES), 1) // width
    own = halves // 2
    levels = vertical_ref.shape[0]
    for level in range(levels):
        for k in range(level, levels):
            weights_ref[level * levels + k] = jnp.broadcast_to(vertical_ref[level : level + 1, k : k + 1], (8, LANES))
    for side, ref in enumerate((own_ref, other_ref)):
        rows_ref[side, :, :sums] = ref[...].astype(F32)
        for p in range(2):
            for first in range(0, halves, planes):
                pieces = []
                for part in range(planes):
                    start = (first + part) * 2 + p
                    pieces.append(rows_ref[side, pl.ds(start, slots, stride=2 * halves), :])
                    if width > slots:
                        pieces.append(jnp.zeros((width - slots, LANES), F32))
                turned = jnp.concatenate(pieces, axis=0).T[:sums]
                rolled = [turned] + [pltpu.roll(turned, d * width, 1) for d in range(1, planes)]
                for part in range(planes):
                    copies = rolled[-part % planes]
                    for plane in range(1, planes):
                        copies = jnp.where(block == plane, rolled[(plane - part) % planes], copies)
                    j = first + part
                    jj = j % own
                    if side == 0:
                        here, there = (jj // 2) * 8 + 6 + jj % 2, jj
                    else:
                        here, there = 8 + jj, 16 + jj
                    start = jnp.where(group == j // own, here, there)
                    out_ref[p, pl.ds(start, sums, stride=24), :] = copies


def add_products(dims, parts, table_ref, rows_ref, p, totals):
    fields, pairs, bands = dims
    band = lax.axis_index("band")
    for i, (side, k) in enumerate(parts):
        first = source(bands, band, k) * pairs
        for q in range(pairs):
            factors = table_ref[p, pl.ds(pl.multiple_of((first + q) * 24, 8), 24), :]
            for f in range(fields):
                row = (f * pairs + q) * 2 + p
                totals[side * fields + f] += rows_ref[i, row : row + 1, :] * factors


def sum_first_kernel(dims, parts, *refs):
    block_refs, (table_ref, total_ref, rows_ref) = refs[:-3], refs[-3:]
    for i, block_ref in enumerate(block_refs):
        rows_ref[i] = block_ref[...].astype(F32)
    for p in range(2):
        totals = [jnp.zeros((24, LANES), F32) for _ in range(2 * dims[0])]
        add_products(dims, parts, table_ref, rows_ref, p, totals)
        for i, total in enumerate(totals):
            total_ref[2 * i + p] = total


def sum_kernel(dims, parts, *refs):
    block_refs, (table_ref, before_ref, total_ref, x_ref, y_ref, xy_ref, rows_ref) = refs[:-7], refs[-7:]
    for i, block_ref in enumerate(block_refs):
        rows_ref[i] = block_ref[...].astype(F32)
    for p in range(2):
        totals = [before_ref[2 * i + p] for i in range(2 * dims[0])]
        add_products(dims, parts, table_ref, rows_ref, p, totals)
        for i, total in enumerate(totals):
            total_ref[2 * i + p] = total
    for at, ref in ((0, x_ref), (8, y_ref), (16, xy_ref)):
        ref[...] = total_ref[:, at : at + 8, :].reshape(ref.shape).astype(BF16)


def finish_kernel(dims, weights_ref, slot_lanes_ref, total_ref, x_ref, y_ref, xy_ref, out_hbm, temps_ref, rows_ref, out_ref, sems):
    fields, levels, halves, slots, waves = dims
    planes = 2 * (levels // 4)
    width = LANES // planes
    lev, group = lax.axis_index("lev"), lax.axis_index("grp")
    y, core = lev // 2, lev % 2
    count = 4 * fields
    from_x, from_y, from_xy = (r[...].astype(F32).reshape(count, 8, LANES) for r in (x_ref, y_ref, xy_ref))
    half = (lev * 2 + group) * halves + iota((8, LANES), 0)
    field_rows = levels * halves * 2
    copies = []

    def store(p, f, level, c, value):
        start = ((p * (fields + 1) + f) * levels + level) * (2 * halves) + c
        rows_ref[pl.ds(start, halves, stride=2), :] = value[:halves]

    def send(p, first, last):
        start, stop = ((p * (fields + 1) + f) * field_rows for f in (first, last))
        out_ref[start:stop] = rows_ref[start:stop, :slots].astype(BF16)
        part = pl.ds(start, stop - start)
        copies.append(pltpu.make_async_copy(out_ref.at[part], out_hbm.at[part], sems.at[len(copies)]))
        copies[-1].start()

    for p in range(2):
        valid = slot_lanes_ref[...] + 2 * half + p <= waves - 1
        for f in range(fields):
            for side in range(2):
                n = (side * fields + f) * 2 + p
                far_n = ((1 - side) * fields + f) * 2 + p
                kept = jnp.concatenate(
                    [total_ref[n, 6:8, :], total_ref[n, 14:16, :], total_ref[n, 22:24, :], jnp.zeros((2, LANES), F32)],
                    axis=0,
                )
                for far, value in enumerate((kept + from_x[n], from_y[far_n] + from_xy[far_n])):
                    value = jnp.where(valid, value, 0.0)
                    first = ((y ^ far) * 2 + (core ^ side)) * (levels // 4)
                    for plane in range(planes):
                        l, c = plane // 2, plane % 2
                        shifted = value if plane == 0 else pltpu.roll(value, LANES - plane * width, 1)
                        store(p, f, first + l, c, shifted)
                        if f == fields - 1:
                            temps_ref[first + l, 2 * p + c] = shifted
        send(p, 0, fields)
    for p in range(2):
        for c in range(2):
            temps = [temps_ref[k, 2 * p + c] for k in range(levels)]
            for level in range(levels):
                value = weights_ref[level * levels + level] * temps[level]
                for k in range(level + 1, levels):
                    value += weights_ref[level * levels + k] * temps[k]
                store(p, fields, level, c, value)
        send(p, fields, fields + 1)
    for copy in copies:
        copy.wait()


HBM = pl.BlockSpec(memory_space=pltpu.HBM)
VMEM = pl.BlockSpec(memory_space=pltpu.VMEM)


def fast_body(fourier, legendre, lat_points, wave_slots, vertical):
    fields, local_levels, _, _, _, pairs, waves = fourier.shape
    slots, _, halves, _, sums = legendre.shape
    bands = lax.axis_size("band")
    levels = 4 * local_levels
    planes = 2 * local_levels
    shape = jax.ShapeDtypeStruct

    functions = legendre.transpose(0, 2, 3, 1, 4).reshape(slots * halves * 2, sums)
    other_functions = flipped(functions, "lev", 3)

    rows = fourier.transpose(0, 1, 2, 4, 5, 3, 6).reshape(-1, waves)
    block = shape((2 * fields * pairs, LANES), BF16)
    slot_lanes, functions, vertical, *blocks = pl.pallas_call(
        functools.partial(prepare_kernel, (fields, planes, pairs, slots, waves)),
        in_specs=[HBM] * 5,
        out_specs=[VMEM] * (3 + bands),
        out_shape=[
            shape((8, LANES), jnp.int32),
            shape(functions.shape, BF16),
            shape(vertical.shape, F32),
        ]
        + [block] * bands,
        scratch_shapes=[
            pltpu.SMEM(lat_points.shape, jnp.int32),
            pltpu.SMEM((1, wave_slots.size), jnp.int32),
            pltpu.VMEM(rows.shape, BF16),
            pltpu.SemaphoreType.DMA((4 + PIECES,)),
        ],
        compiler_params=pltpu.CompilerParams(vmem_limit_bytes=GRANT),
        name="prepare",
    )(*[pltpu.with_memory_space_constraint(v, pltpu.HBM) for v in (lat_points, wave_slots.reshape(1, -1), rows, functions, vertical)])

    steps = tuple(range(1, bands))
    own = {0: blocks[0]}
    for k in steps:
        own[k] = lax.ppermute(blocks[k], ("band", "lev"), crossed(k))
    table, weights = pl.pallas_call(
        functools.partial(spread_kernel, (planes, slots, halves, sums)),
        in_specs=[VMEM] * 3,
        out_specs=[VMEM] * 2,
        out_shape=[shape((2, sums * 24, LANES), F32), shape((levels * levels, 8, LANES), F32)],
        scratch_shapes=[pltpu.VMEM((2, slots * halves * 2, LANES), F32)],
        compiler_params=pltpu.CompilerParams(vmem_limit_bytes=GRANT),
        name="spread",
    )(functions, other_functions, vertical)
    other = {}
    for k in (0, *steps):
        other[k] = flipped(own[k], "lev", 1)

    count = 4 * fields
    message = shape((count * 8, LANES), BF16)
    totals = shape((count, 24, LANES), F32)
    parts = [(own[k], (min(k, 1), k)) for k in range(bands)] + [(other[k], (1 - min(k, 1), k)) for k in range(bands)]
    early, late = parts[: bands + 2], parts[bands + 2 :]
    before = pl.pallas_call(
        functools.partial(sum_first_kernel, (fields, pairs, bands), [where for _, where in early]),
        in_specs=[VMEM] * (len(early) + 1),
        out_specs=VMEM,
        out_shape=totals,
        scratch_shapes=[pltpu.VMEM((len(early), *block.shape), F32)],
        compiler_params=pltpu.CompilerParams(vmem_limit_bytes=GRANT),
        name="sum_first",
    )(*[value for value, _ in early], table)
    total, to_x, to_y, to_xy = pl.pallas_call(
        functools.partial(sum_kernel, (fields, pairs, bands), [where for _, where in late]),
        in_specs=[VMEM] * (len(late) + 2),
        out_specs=[VMEM] * 4,
        out_shape=[totals] + [message] * 3,
        scratch_shapes=[pltpu.VMEM((max(len(late), 1), *block.shape), F32)],
        compiler_params=pltpu.CompilerParams(vmem_limit_bytes=GRANT),
        name="sum",
    )(*[value for value, _ in late], table, before)

    from_xy = lax.ppermute(to_xy, ("lev", "grp"), [(i, i ^ 7) for i in range(8)])
    from_x = flipped(to_x, "grp", 1)
    from_y = flipped(to_y, "lev", 3)
    own_halves = halves // 2
    out_rows = 2 * (fields + 1) * levels * own_halves * 2
    out = pl.pallas_call(
        functools.partial(finish_kernel, (fields, levels, own_halves, slots, waves)),
        in_specs=[VMEM] * 6,
        out_specs=HBM,
        out_shape=shape((out_rows, slots), BF16),
        scratch_shapes=[
            pltpu.VMEM((levels, 4, 8, LANES), F32),
            pltpu.VMEM((out_rows, LANES), F32),
            pltpu.VMEM((out_rows, slots), BF16),
            pltpu.SemaphoreType.DMA((4,)),
        ],
        compiler_params=pltpu.CompilerParams(vmem_limit_bytes=GRANT),
        name="finish",
    )(weights, slot_lanes, total, from_x, from_y, from_xy)
    out = out.reshape(2, fields + 1, levels, own_halves, 2, slots)
    return out.transpose(5, 0, 1, 2, 4, 3)


def fits(mesh, fourier, legendre):
    bands, levs, groups = (mesh.shape[a] for a in ("band", "lev", "grp"))
    fields, levels, _, _, _, pairs, waves = fourier.shape
    slots, _, halves, _, sums = legendre.shape
    planes = 2 * levels // levs
    return (
        levs == 4
        and groups == 2
        and bands & (bands - 1) == 0
        and waves <= LANES
        and sums <= LANES
        and halves // levs == 12
        and LANES % planes == 0
        and 12 % planes == 0
        and slots // bands <= LANES // planes
        and slots // bands % 8 == 0
        and 2 * pairs // bands % 8 == 0
        and sums % 8 == 0
        and fields * planes * 2 * (pairs // bands) % (16 * PIECES) == 0
    )


def general_body(fourier, legendre, lat_points, wave_slots, vertical):
    wave_count = fourier.shape[6]
    cutoff = jnp.minimum(wave_count - 1, (lat_points - 1) // 2)
    wave_ids = lax.broadcasted_iota(jnp.int32, (1, 1, wave_count), 2)
    kept_mask = wave_ids <= cutoff[:, :, None]
    masked = jnp.where(kept_mask, fourier, jnp.zeros((), fourier.dtype))
    slot_table = (
        wave_slots[:, None] == lax.broadcasted_iota(jnp.int32, (wave_count, wave_count), 1)
    ).astype(jnp.bfloat16)
    ordered = lax.dot_general(
        slot_table, masked, (((1,), (6,)), ((), ())), preferred_element_type=jnp.float32
    ).astype(jnp.bfloat16)
    at_owners = lax.all_to_all(ordered, "band", split_axis=0, concat_axis=6, tiled=True)
    coeffs = lax.all_gather(at_owners, "lev", axis=2, tiled=True)
    level_count = coeffs.shape[2]
    level_rows = lax.broadcasted_iota(jnp.int32, (level_count, level_count), 0)
    level_cols = lax.broadcasted_iota(jnp.int32, (level_count, level_count), 1)
    integral = jnp.where(level_cols >= level_rows, vertical, jnp.zeros((), vertical.dtype))
    geopotential = jnp.einsum(
        "lk,skchgr->slchgr",
        integral,
        coeffs[:, 2].astype(jnp.float32),
        precision=lax.Precision.HIGHEST,
    ).astype(jnp.bfloat16)
    fields = jnp.concatenate([coeffs, geopotential[:, None]], axis=1)
    northern = fields[:, :, :, :, 0].astype(jnp.float32)
    southern = fields[:, :, :, :, 1].astype(jnp.float32)
    parity = jnp.stack(
        [(northern + southern).astype(jnp.bfloat16), (northern - southern).astype(jnp.bfloat16)],
        axis=4,
    )
    partial_value = lax.dot_general(
        parity, legendre, (((5, 6), (3, 4)), ((0, 4), (0, 1))), preferred_element_type=jnp.float32
    )
    groups = lax.axis_size("grp")
    half_count = partial_value.shape[5] // groups
    me = lax.axis_index("grp")
    summed = lax.dynamic_slice_in_dim(partial_value, me * half_count, half_count, 5)
    for step in range(1, groups):
        target = lax.rem(me + step, groups)
        piece = lax.dynamic_slice_in_dim(partial_value, target * half_count, half_count, 5)
        summed = summed + lax.ppermute(
            piece, "grp", [(i, (i + step) % groups) for i in range(groups)]
        )
    slot_count = summed.shape[0]
    slot_waves = lax.dynamic_slice_in_dim(
        wave_slots, lax.axis_index("band") * slot_count, slot_count
    )
    block_start = (lax.axis_index("lev") * groups + me) * half_count
    half_ids = block_start + lax.broadcasted_iota(jnp.int32, (1, 1, half_count), 2)
    parity_ids = lax.broadcasted_iota(jnp.int32, (1, 2, 1), 1)
    total = slot_waves[:, None, None] + 2 * half_ids + parity_ids
    valid = (total <= wave_count - 1)[:, :, None, None, None, :]
    return jnp.where(valid, summed, 0.0).astype(jnp.bfloat16)


def solution(mesh):
    def program(fourier, legendre, lat_points, wave_slots, vertical):
        placed = (
            P(None, "lev", None, None, "grp", "band", None),
            P("band", None, "lev", "grp", None),
            P("grp", "band"),
            P(),
            P(),
        )
        fast = fits(mesh, fourier, legendre)
        step = jax.shard_map(
            fast_body if fast else general_body,
            mesh=mesh,
            in_specs=placed,
            out_specs=P("band", None, None, None, None, ("lev", "grp")),
            check_vma=False,
        )
        return step(fourier, legendre, lat_points, wave_slots, vertical)

    return program
```

```python
import functools

import jax
import jax.numpy as jnp
from jax import lax
from jax.experimental import pallas as pl
from jax.experimental.pallas import tpu as pltpu
from jax.sharding import PartitionSpec as P

F32, BF16 = jnp.float32, jnp.bfloat16
LANES = 128
GRANT = 8 << 20
PIECES = 3


def flipped(value, axis, step):
    return lax.ppermute(value, axis, [(i, i ^ step) for i in range(lax.axis_size(axis))])


def rounds(bands):
    if bands == 4:
        return ((2, 3, 1, 0), (3, 2, 0, 1), (1, 0, 3, 2))
    return tuple(tuple((b + k) % bands for b in range(bands)) for k in range(1, bands))


def picked(table, index):
    value = jnp.int32(table[0])
    for i in range(1, len(table)):
        value = jnp.where(index == i, table[i], value)
    return value


def target(bands, band, k):
    return picked(rounds(bands)[k - 1], band) if k else band


def source(bands, band, k):
    return picked([rounds(bands)[k - 1].index(b) for b in range(bands)], band) if k else band


def crossed(k):
    bands, levs = lax.axis_size("band"), lax.axis_size("lev")
    to = rounds(bands)[k - 1]
    return [(b * levs + v, to[b] * levs + (v ^ 1)) for b in range(bands) for v in range(levs)]


def round_the_square(levs, late):
    return [(v * 2 + g, ((v ^ 1) if g == late else (v ^ 3)) * 2 + 1 - g) for v in range(levs) for g in range(2)]


def iota(shape, dim):
    return lax.broadcasted_iota(jnp.int32, shape, dim)


def prepare_kernel(dims, lat_hbm, slots_hbm, x_hbm, functions_hbm, vertical_hbm, slot_lanes_ref, functions_ref, vertical_ref, *rest):
    fields, planes, pairs, slots, waves = dims
    block_refs, (lat_ref, slots_ref, x_ref, sems) = rest[:-4], rest[-4:]
    width = LANES // planes
    band = lax.axis_index("band")
    share = x_ref.shape[0] // PIECES
    pieces = [pl.ds(i * share, share) for i in range(PIECES)]
    copies = [
        pltpu.make_async_copy(given, held, sems.at[i])
        for i, (given, held) in enumerate(
            (
                (slots_hbm, slots_ref),
                (lat_hbm, lat_ref),
                *((x_hbm.at[piece], x_ref.at[piece]) for piece in pieces),
                (functions_hbm, functions_ref),
                (vertical_hbm, vertical_ref),
            )
        )
    ]
    for copy in copies:
        copy.start()
    lane = iota((8, LANES), 1)
    copies[0].wait()
    tables = []
    for k in range(len(block_refs)):
        first = target(len(block_refs), band, k) * slots
        held = jnp.full((8, LANES), -1, jnp.int32)
        for s in range(slots):
            held = jnp.where(lane % width == s, slots_ref[0, first + s], held)
        if k == 0:
            slot_lanes_ref[...] = held
        hot = iota((waves, LANES), 0) == held[0:1]
        tables.append(jnp.where(hot, 1.0, 0.0).astype(BF16))
    pair_rows = iota((2 * pairs, waves), 0) >> 1
    points = jnp.zeros((2 * pairs, waves), jnp.int32)
    copies[1].wait()
    for q in range(pairs):
        points = jnp.where(pair_rows == q, lat_ref[0, q], points)
    cutoff = jnp.minimum(waves - 1, (points - 1) >> 1)
    kept = iota((2 * pairs, waves), 1) <= cutoff
    for copy in copies[2 : 2 + PIECES]:
        copy.wait()
    x = x_ref[...].astype(F32)
    rows = x.shape[0]
    following = pltpu.roll(x, rows - 1, 0)
    previous = pltpu.roll(x, 1, 0)
    north = (iota(x.shape, 0) & 1) == 0
    parity = jnp.where(north, x + following, previous - x)
    parity = parity.reshape(fields * planes, 2 * pairs, waves)
    parity = jnp.where(kept[None], parity, 0.0)
    by_plane = jnp.concatenate(
        [parity[f * planes + plane] for plane in range(planes) for f in range(fields)], axis=0
    ).astype(BF16)
    chosen = jnp.dot(by_plane, jnp.concatenate(tables, axis=1), preferred_element_type=F32)
    count = 2 * fields * pairs
    plane_of = iota((count, LANES), 1) // width
    for k, block_ref in enumerate(block_refs):
        mine = chosen[:, k * LANES : (k + 1) * LANES]
        block = mine[:count]
        for plane in range(1, planes):
            block = jnp.where(plane_of == plane, mine[plane * count : (plane + 1) * count], block)
        block_ref[...] = block.astype(BF16)
    for copy in copies[2 + PIECES :]:
        copy.wait()


def spread_kernel(dims, own_ref, core_ref, other_ref, vertical_ref, out_ref, weights_ref, rows_ref):
    planes, slots, halves, sums = dims
    width = LANES // planes
    group = lax.axis_index("grp")
    block = iota((sums, LANES), 1) // width
    own = halves // 2
    levels = vertical_ref.shape[0]
    for level in range(levels):
        for k in range(level, levels):
            weights_ref[level * levels + k] = jnp.broadcast_to(vertical_ref[level : level + 1, k : k + 1], (8, LANES))
    for side, ref in enumerate((own_ref, other_ref, core_ref)):
        rows_ref[side, :, :sums] = ref[...].astype(F32)
    for side in range(2):
        for p in range(2):
            for first in range(0, halves, planes):
                pieces = []
                for part in range(planes):
                    start = (first + part) * 2 + p
                    piece = rows_ref[side, pl.ds(start, slots, stride=2 * halves), :]
                    if side == 0:
                        across = rows_ref[2, pl.ds(start, slots, stride=2 * halves), :]
                        piece = jnp.where(group == (first + part) // own, piece, across)
                    pieces.append(piece)
                    if width > slots:
                        pieces.append(jnp.zeros((width - slots, LANES), F32))
                turned = jnp.concatenate(pieces, axis=0).T[:sums]
                rolled = [turned] + [pltpu.roll(turned, d * width, 1) for d in range(1, planes)]
                for part in range(planes):
                    copies = rolled[-part % planes]
                    for plane in range(1, planes):
                        copies = jnp.where(block == plane, rolled[(plane - part) % planes], copies)
                    j = first + part
                    jj = j % own
                    if side == 0:
                        here, there = (jj // 2) * 8 + 6 + jj % 2, jj
                    else:
                        here, there = 8 + jj, 16 + jj
                    start = jnp.where(group == j // own, here, there)
                    out_ref[p, pl.ds(start, sums, stride=24), :] = copies


def add_products(dims, parts, table_ref, rows_ref, p, totals):
    fields, pairs, bands = dims
    band = lax.axis_index("band")
    for i, (side, k) in enumerate(parts):
        first = source(bands, band, k) * pairs
        for q in range(pairs):
            factors = table_ref[p, pl.ds(pl.multiple_of((first + q) * 24, 8), 24), :]
            for f in range(fields):
                row = (f * pairs + q) * 2 + p
                totals[side * fields + f] += rows_ref[i, row : row + 1, :] * factors


def sum_first_kernel(dims, parts, *refs):
    block_refs, (table_ref, total_ref, rows_ref) = refs[:-3], refs[-3:]
    for i, block_ref in enumerate(block_refs):
        rows_ref[i] = block_ref[...].astype(F32)
    for p in range(2):
        totals = [jnp.zeros((24, LANES), F32) for _ in range(2 * dims[0])]
        add_products(dims, parts, table_ref, rows_ref, p, totals)
        for i, total in enumerate(totals):
            total_ref[2 * i + p] = total


def sum_kernel(dims, parts, *refs):
    block_refs, (table_ref, before_ref, total_ref, soon_ref, y_ref, late_ref, rows_ref) = refs[:-7], refs[-7:]
    for i, block_ref in enumerate(block_refs):
        rows_ref[i] = block_ref[...].astype(F32)
    for p in range(2):
        totals = [before_ref[2 * i + p] for i in range(2 * dims[0])]
        add_products(dims, parts, table_ref, rows_ref, p, totals)
        for i, total in enumerate(totals):
            total_ref[2 * i + p] = total
    group = lax.axis_index("grp")
    for at, ref in ((16 * group, soon_ref), (8, y_ref), (16 - 16 * group, late_ref)):
        ref[...] = total_ref[:, pl.ds(pl.multiple_of(at, 8), 8), :].reshape(ref.shape).astype(BF16)


def finish_kernel(dims, weights_ref, slot_lanes_ref, total_ref, soon_ref, y_ref, late_ref, out_hbm, temps_ref, rows_ref, out_ref, sems):
    fields, levels, halves, slots, waves = dims
    planes = 2 * (levels // 4)
    width = LANES // planes
    lev, group = lax.axis_index("lev"), lax.axis_index("grp")
    y, core = lev // 2, lev % 2
    count = 4 * fields
    soon, from_y, late = (r[...].astype(F32).reshape(count, 8, LANES) for r in (soon_ref, y_ref, late_ref))
    from_x, from_xy = jnp.where(group == 0, late, soon), jnp.where(group == 0, soon, late)
    half = (lev * 2 + group) * halves + iota((8, LANES), 0)
    field_rows = levels * halves * 2
    copies = []

    def store(p, f, level, c, value):
        start = ((p * (fields + 1) + f) * levels + level) * (2 * halves) + c
        rows_ref[pl.ds(start, halves, stride=2), :] = value[:halves]

    def send(p, first, last):
        start, stop = ((p * (fields + 1) + f) * field_rows for f in (first, last))
        out_ref[start:stop] = rows_ref[start:stop, :slots].astype(BF16)
        part = pl.ds(start, stop - start)
        copies.append(pltpu.make_async_copy(out_ref.at[part], out_hbm.at[part], sems.at[len(copies)]))
        copies[-1].start()

    for p in range(2):
        valid = slot_lanes_ref[...] + 2 * half + p <= waves - 1
        for f in range(fields):
            for side in range(2):
                n = (side * fields + f) * 2 + p
                far_n = ((1 - side) * fields + f) * 2 + p
                kept = jnp.concatenate(
                    [total_ref[n, 6:8, :], total_ref[n, 14:16, :], total_ref[n, 22:24, :], jnp.zeros((2, LANES), F32)],
                    axis=0,
                )
                for far, value in enumerate((kept + from_x[far_n], from_y[far_n] + from_xy[far_n])):
                    value = jnp.where(valid, value, 0.0)
                    first = ((y ^ far) * 2 + (core ^ side)) * (levels // 4)
                    for plane in range(planes):
                        l, c = plane // 2, plane % 2
                        shifted = value if plane == 0 else pltpu.roll(value, LANES - plane * width, 1)
                        store(p, f, first + l, c, shifted)
                        if f == fields - 1:
                            temps_ref[first + l, 2 * p + c] = shifted
        send(p, 0, fields)
    for p in range(2):
        for c in range(2):
            temps = [temps_ref[k, 2 * p + c] for k in range(levels)]
            for level in range(levels):
                value = weights_ref[level * levels + level] * temps[level]
                for k in range(level + 1, levels):
                    value += weights_ref[level * levels + k] * temps[k]
                store(p, fields, level, c, value)
        send(p, fields, fields + 1)
    for copy in copies:
        copy.wait()


HBM = pl.BlockSpec(memory_space=pltpu.HBM)
VMEM = pl.BlockSpec(memory_space=pltpu.VMEM)


def fast_body(fourier, legendre, lat_points, wave_slots, vertical):
    fields, local_levels, _, _, _, pairs, waves = fourier.shape
    slots, _, halves, _, sums = legendre.shape
    bands = lax.axis_size("band")
    levels = 4 * local_levels
    planes = 2 * local_levels
    shape = jax.ShapeDtypeStruct

    functions = legendre.transpose(0, 2, 3, 1, 4).reshape(slots * halves * 2, sums)
    other_functions = flipped(functions, "lev", 3)

    rows = fourier.transpose(0, 1, 2, 4, 5, 3, 6).reshape(-1, waves)
    block = shape((2 * fields * pairs, LANES), BF16)
    slot_lanes, functions, vertical, *blocks = pl.pallas_call(
        functools.partial(prepare_kernel, (fields, planes, pairs, slots, waves)),
        in_specs=[HBM] * 5,
        out_specs=[VMEM] * (3 + bands),
        out_shape=[
            shape((8, LANES), jnp.int32),
            shape(functions.shape, BF16),
            shape(vertical.shape, F32),
        ]
        + [block] * bands,
        scratch_shapes=[
            pltpu.SMEM(lat_points.shape, jnp.int32),
            pltpu.SMEM((1, wave_slots.size), jnp.int32),
            pltpu.VMEM(rows.shape, BF16),
            pltpu.SemaphoreType.DMA((4 + PIECES,)),
        ],
        compiler_params=pltpu.CompilerParams(vmem_limit_bytes=GRANT),
        name="prepare",
    )(*[pltpu.with_memory_space_constraint(v, pltpu.HBM) for v in (lat_points, wave_slots.reshape(1, -1), rows, functions, vertical)])

    steps = tuple(range(1, bands))
    own = {0: blocks[0]}
    for k in steps:
        own[k] = lax.ppermute(blocks[k], ("band", "lev"), crossed(k))
    core_functions = flipped(functions, "lev", 1)
    table, weights = pl.pallas_call(
        functools.partial(spread_kernel, (planes, slots, halves, sums)),
        in_specs=[VMEM] * 4,
        out_specs=[VMEM] * 2,
        out_shape=[shape((2, sums * 24, LANES), F32), shape((levels * levels, 8, LANES), F32)],
        scratch_shapes=[pltpu.VMEM((3, slots * halves * 2, LANES), F32)],
        compiler_params=pltpu.CompilerParams(vmem_limit_bytes=GRANT),
        name="spread",
    )(functions, core_functions, other_functions, vertical)
    other = {}
    for k in (0, *steps):
        other[k] = flipped(own[k], "lev", 1)

    count = 4 * fields
    message = shape((count * 8, LANES), BF16)
    totals = shape((count, 24, LANES), F32)
    parts = [(own[k], (min(k, 1), k)) for k in range(bands)] + [(other[k], (1 - min(k, 1), k)) for k in range(bands)]
    early, others = parts[: bands + 2], parts[bands + 2 :]
    before = pl.pallas_call(
        functools.partial(sum_first_kernel, (fields, pairs, bands), [where for _, where in early]),
        in_specs=[VMEM] * (len(early) + 1),
        out_specs=VMEM,
        out_shape=totals,
        scratch_shapes=[pltpu.VMEM((len(early), *block.shape), F32)],
        compiler_params=pltpu.CompilerParams(vmem_limit_bytes=GRANT),
        name="sum_first",
    )(*[value for value, _ in early], table)
    total, soon, to_y, late = pl.pallas_call(
        functools.partial(sum_kernel, (fields, pairs, bands), [where for _, where in others]),
        in_specs=[VMEM] * (len(others) + 2),
        out_specs=[VMEM] * 4,
        out_shape=[totals] + [message] * 3,
        scratch_shapes=[pltpu.VMEM((max(len(others), 1), *block.shape), F32)],
        compiler_params=pltpu.CompilerParams(vmem_limit_bytes=GRANT),
        name="sum",
    )(*[value for value, _ in others], table, before)

    levs = lax.axis_size("lev")
    from_soon = lax.ppermute(soon, ("lev", "grp"), round_the_square(levs, 0))
    from_y = flipped(to_y, "lev", 3)
    from_late = lax.ppermute(late, ("lev", "grp"), round_the_square(levs, 1))
    own_halves = halves // 2
    out_rows = 2 * (fields + 1) * levels * own_halves * 2
    out = pl.pallas_call(
        functools.partial(finish_kernel, (fields, levels, own_halves, slots, waves)),
        in_specs=[VMEM] * 6,
        out_specs=HBM,
        out_shape=shape((out_rows, slots), BF16),
        scratch_shapes=[
            pltpu.VMEM((levels, 4, 8, LANES), F32),
            pltpu.VMEM((out_rows + 16, LANES), F32),
            pltpu.VMEM((out_rows, slots), BF16),
            pltpu.SemaphoreType.DMA((4,)),
        ],
        compiler_params=pltpu.CompilerParams(vmem_limit_bytes=GRANT),
        name="finish",
    )(weights, slot_lanes, total, from_soon, from_y, from_late)
    out = out.reshape(2, fields + 1, levels, own_halves, 2, slots)
    return out.transpose(5, 0, 1, 2, 4, 3)


def fits(mesh, fourier, legendre):
    bands, levs, groups = (mesh.shape[a] for a in ("band", "lev", "grp"))
    fields, levels, _, _, _, pairs, waves = fourier.shape
    slots, _, halves, _, sums = legendre.shape
    planes = 2 * levels // levs
    return (
        levs == 4
        and groups == 2
        and bands & (bands - 1) == 0
        and waves <= LANES
        and sums <= LANES
        and halves // levs == 12
        and LANES % planes == 0
        and 12 % planes == 0
        and slots // bands <= LANES // planes
        and slots // bands % 8 == 0
        and 2 * pairs // bands % 8 == 0
        and sums % 8 == 0
        and fields * planes * 2 * (pairs // bands) % (16 * PIECES) == 0
    )


def general_body(fourier, legendre, lat_points, wave_slots, vertical):
    wave_count = fourier.shape[6]
    cutoff = jnp.minimum(wave_count - 1, (lat_points - 1) // 2)
    wave_ids = lax.broadcasted_iota(jnp.int32, (1, 1, wave_count), 2)
    kept_mask = wave_ids <= cutoff[:, :, None]
    masked = jnp.where(kept_mask, fourier, jnp.zeros((), fourier.dtype))
    slot_table = (
        wave_slots[:, None] == lax.broadcasted_iota(jnp.int32, (wave_count, wave_count), 1)
    ).astype(jnp.bfloat16)
    ordered = lax.dot_general(
        slot_table, masked, (((1,), (6,)), ((), ())), preferred_element_type=jnp.float32
    ).astype(jnp.bfloat16)
    at_owners = lax.all_to_all(ordered, "band", split_axis=0, concat_axis=6, tiled=True)
    coeffs = lax.all_gather(at_owners, "lev", axis=2, tiled=True)
    level_count = coeffs.shape[2]
    level_rows = lax.broadcasted_iota(jnp.int32, (level_count, level_count), 0)
    level_cols = lax.broadcasted_iota(jnp.int32, (level_count, level_count), 1)
    integral = jnp.where(level_cols >= level_rows, vertical, jnp.zeros((), vertical.dtype))
    geopotential = jnp.einsum(
        "lk,skchgr->slchgr",
        integral,
        coeffs[:, 2].astype(jnp.float32),
        precision=lax.Precision.HIGHEST,
    ).astype(jnp.bfloat16)
    fields = jnp.concatenate([coeffs, geopotential[:, None]], axis=1)
    northern = fields[:, :, :, :, 0].astype(jnp.float32)
    southern = fields[:, :, :, :, 1].astype(jnp.float32)
    parity = jnp.stack(
        [(northern + southern).astype(jnp.bfloat16), (northern - southern).astype(jnp.bfloat16)],
        axis=4,
    )
    partial_value = lax.dot_general(
        parity, legendre, (((5, 6), (3, 4)), ((0, 4), (0, 1))), preferred_element_type=jnp.float32
    )
    groups = lax.axis_size("grp")
    half_count = partial_value.shape[5] // groups
    me = lax.axis_index("grp")
    summed = lax.dynamic_slice_in_dim(partial_value, me * half_count, half_count, 5)
    for step in range(1, groups):
        target = lax.rem(me + step, groups)
        piece = lax.dynamic_slice_in_dim(partial_value, target * half_count, half_count, 5)
        summed = summed + lax.ppermute(
            piece, "grp", [(i, (i + step) % groups) for i in range(groups)]
        )
    slot_count = summed.shape[0]
    slot_waves = lax.dynamic_slice_in_dim(
        wave_slots, lax.axis_index("band") * slot_count, slot_count
    )
    block_start = (lax.axis_index("lev") * groups + me) * half_count
    half_ids = block_start + lax.broadcasted_iota(jnp.int32, (1, 1, half_count), 2)
    parity_ids = lax.broadcasted_iota(jnp.int32, (1, 2, 1), 1)
    total = slot_waves[:, None, None] + 2 * half_ids + parity_ids
    valid = (total <= wave_count - 1)[:, :, None, None, None, :]
    return jnp.where(valid, summed, 0.0).astype(jnp.bfloat16)


def solution(mesh):
    def program(fourier, legendre, lat_points, wave_slots, vertical):
        placed = (
            P(None, "lev", None, None, "grp", "band", None),
            P("band", None, "lev", "grp", None),
            P("grp", "band"),
            P(),
            P(),
        )
        fast = fits(mesh, fourier, legendre)
        step = jax.shard_map(
            fast_body if fast else general_body,
            mesh=mesh,
            in_specs=placed,
            out_specs=P("band", None, None, None, None, ("lev", "grp")),
            check_vma=False,
        )
        return step(fourier, legendre, lat_points, wave_slots, vertical)

    return program
```

```python
import functools

import jax
import jax.numpy as jnp
from jax import lax
from jax.experimental import pallas as pl
from jax.experimental.pallas import tpu as pltpu
from jax.sharding import PartitionSpec as P

F32, BF16 = jnp.float32, jnp.bfloat16
LANES = 128
GRANT = 8 << 20
PIECES = 3


def flipped(value, axis, step):
    return lax.ppermute(value, axis, [(i, i ^ step) for i in range(lax.axis_size(axis))])


def rounds(bands):
    if bands == 4:
        return ((2, 3, 1, 0), (3, 2, 0, 1), (1, 0, 3, 2))
    return tuple(tuple((b + k) % bands for b in range(bands)) for k in range(1, bands))


def picked(table, index):
    value = jnp.int32(table[0])
    for i in range(1, len(table)):
        value = jnp.where(index == i, table[i], value)
    return value


def target(bands, band, k):
    return picked(rounds(bands)[k - 1], band) if k else band


def source(bands, band, k):
    return picked([rounds(bands)[k - 1].index(b) for b in range(bands)], band) if k else band


def crossed(k):
    bands, levs = lax.axis_size("band"), lax.axis_size("lev")
    to = rounds(bands)[k - 1]
    return [(b * levs + v, to[b] * levs + (v ^ 1)) for b in range(bands) for v in range(levs)]


def round_the_square(levs, late):
    return [(v * 2 + g, ((v ^ 1) if g == late else (v ^ 3)) * 2 + 1 - g) for v in range(levs) for g in range(2)]


def iota(shape, dim):
    return lax.broadcasted_iota(jnp.int32, shape, dim)


def prepare_kernel(dims, lat_hbm, slots_hbm, x_hbm, functions_hbm, vertical_hbm, slot_lanes_ref, functions_ref, vertical_ref, *rest):
    fields, planes, pairs, slots, waves = dims
    block_refs, (lat_ref, slots_ref, x_ref, sems) = rest[:-4], rest[-4:]
    width = LANES // planes
    band = lax.axis_index("band")
    share = x_ref.shape[0] // PIECES
    pieces = [pl.ds(i * share, share) for i in range(PIECES)]
    copies = [
        pltpu.make_async_copy(given, held, sems.at[i])
        for i, (given, held) in enumerate(
            (
                (slots_hbm, slots_ref),
                (lat_hbm, lat_ref),
                *((x_hbm.at[piece], x_ref.at[piece]) for piece in pieces),
                (functions_hbm, functions_ref),
                (vertical_hbm, vertical_ref),
            )
        )
    ]
    for copy in copies:
        copy.start()
    lane = iota((8, LANES), 1)
    copies[0].wait()
    tables = []
    for k in range(len(block_refs)):
        first = target(len(block_refs), band, k) * slots
        held = jnp.full((8, LANES), -1, jnp.int32)
        for s in range(slots):
            held = jnp.where(lane % width == s, slots_ref[0, first + s], held)
        if k == 0:
            slot_lanes_ref[...] = held
        hot = iota((waves, LANES), 0) == held[0:1]
        tables.append(jnp.where(hot, 1.0, 0.0).astype(BF16))
    pair_rows = iota((2 * pairs, waves), 0) >> 1
    points = jnp.zeros((2 * pairs, waves), jnp.int32)
    copies[1].wait()
    for q in range(pairs):
        points = jnp.where(pair_rows == q, lat_ref[0, q], points)
    cutoff = jnp.minimum(waves - 1, (points - 1) >> 1)
    kept = iota((2 * pairs, waves), 1) <= cutoff
    for copy in copies[2 : 2 + PIECES]:
        copy.wait()
    x = x_ref[...].astype(F32)
    rows = x.shape[0]
    following = pltpu.roll(x, rows - 1, 0)
    previous = pltpu.roll(x, 1, 0)
    north = (iota(x.shape, 0) & 1) == 0
    parity = jnp.where(north, x + following, previous - x)
    parity = parity.reshape(fields * planes, 2 * pairs, waves)
    parity = jnp.where(kept[None], parity, 0.0)
    by_plane = jnp.concatenate(
        [parity[f * planes + plane] for plane in range(planes) for f in range(fields)], axis=0
    ).astype(BF16)
    chosen = jnp.dot(by_plane, jnp.concatenate(tables, axis=1), preferred_element_type=F32)
    count = 2 * fields * pairs
    plane_of = iota((count, LANES), 1) // width
    for k, block_ref in enumerate(block_refs):
        mine = chosen[:, k * LANES : (k + 1) * LANES]
        block = mine[:count]
        for plane in range(1, planes):
            block = jnp.where(plane_of == plane, mine[plane * count : (plane + 1) * count], block)
        block_ref[...] = block.astype(BF16)
    for copy in copies[2 + PIECES :]:
        copy.wait()


def spread_kernel(dims, own_ref, core_ref, other_ref, vertical_ref, out_ref, weights_ref, rows_ref):
    planes, slots, halves, sums = dims
    width = LANES // planes
    group = lax.axis_index("grp")
    block = iota((sums, LANES), 1) // width
    own = halves // 2
    levels = vertical_ref.shape[0]
    for level in range(levels):
        for k in range(level, levels):
            weights_ref[level * levels + k] = jnp.broadcast_to(vertical_ref[level : level + 1, k : k + 1], (8, LANES))
    for side, ref in enumerate((own_ref, other_ref, core_ref)):
        rows_ref[side, :, :sums] = ref[...].astype(F32)
    for side in range(2):
        for p in range(2):
            for first in range(0, halves, planes):
                pieces = []
                for part in range(planes):
                    start = (first + part) * 2 + p
                    piece = rows_ref[side, pl.ds(start, slots, stride=2 * halves), :]
                    if side == 0:
                        across = rows_ref[2, pl.ds(start, slots, stride=2 * halves), :]
                        piece = jnp.where(group == (first + part) // own, piece, across)
                    pieces.append(piece)
                    if width > slots:
                        pieces.append(jnp.zeros((width - slots, LANES), F32))
                turned = jnp.concatenate(pieces, axis=0).T[:sums]
                rolled = [turned] + [pltpu.roll(turned, d * width, 1) for d in range(1, planes)]
                for part in range(planes):
                    copies = rolled[-part % planes]
                    for plane in range(1, planes):
                        copies = jnp.where(block == plane, rolled[(plane - part) % planes], copies)
                    j = first + part
                    jj = j % own
                    if side == 0:
                        here, there = (jj // 2) * 8 + 6 + jj % 2, jj
                    else:
                        here, there = 8 + jj, 16 + jj
                    start = jnp.where(group == j // own, here, there)
                    out_ref[p, pl.ds(start, sums, stride=24), :] = copies


def add_products(dims, parts, table_ref, rows_ref, p, totals):
    fields, pairs, bands = dims
    band = lax.axis_index("band")
    for i, (side, k) in enumerate(parts):
        first = source(bands, band, k) * pairs
        for q in range(pairs):
            factors = table_ref[p, pl.ds(pl.multiple_of((first + q) * 24, 8), 24), :]
            for f in range(fields):
                row = (f * pairs + q) * 2 + p
                totals[side * fields + f] += rows_ref[i, row : row + 1, :] * factors


def sum_first_kernel(dims, parts, *refs):
    block_refs, (table_ref, total_ref, rows_ref) = refs[:-3], refs[-3:]
    for i, block_ref in enumerate(block_refs):
        rows_ref[i] = block_ref[...].astype(F32)
    for p in range(2):
        totals = [jnp.zeros((24, LANES), F32) for _ in range(2 * dims[0])]
        add_products(dims, parts, table_ref, rows_ref, p, totals)
        for i, total in enumerate(totals):
            total_ref[2 * i + p] = total


def sum_kernel(dims, parts, *refs):
    block_refs, (table_ref, before_ref, total_ref, soon_ref, y_ref, late_ref, rows_ref, packed_ref) = refs[:-8], refs[-8:]
    for i, block_ref in enumerate(block_refs):
        rows_ref[i] = block_ref[...].astype(F32)
    for p in range(2):
        totals = [before_ref[2 * i + p] for i in range(2 * dims[0])]
        add_products(dims, parts, table_ref, rows_ref, p, totals)
        for i, total in enumerate(totals):
            total_ref[2 * i + p] = total
    group = lax.axis_index("grp")
    halves = packed_ref.shape[1] // total_ref.shape[0]
    for i, (at, ref) in enumerate(((16 * group, soon_ref), (8, y_ref), (16 - 16 * group, late_ref))):
        for n in range(total_ref.shape[0]):
            packed_ref[i, n * halves : (n + 1) * halves] = total_ref[n, pl.ds(pl.multiple_of(at, 8), halves), :]
        ref[...] = packed_ref[i].astype(BF16)


def finish_kernel(dims, weights_ref, slot_lanes_ref, total_ref, soon_ref, y_ref, late_ref, out_hbm, temps_ref, rows_ref, out_ref, given_ref, sems):
    fields, levels, halves, slots, waves = dims
    planes = 2 * (levels // 4)
    width = LANES // planes
    lev, group = lax.axis_index("lev"), lax.axis_index("grp")
    y, core = lev // 2, lev % 2
    count = 4 * fields
    for i, ref in enumerate((soon_ref, y_ref, late_ref)):
        given_ref[i, : count * halves] = ref[...].astype(F32)

    def given(i, n):
        return given_ref[i, n * halves : n * halves + 8, :]

    half = (lev * 2 + group) * halves + iota((8, LANES), 0)
    field_rows = levels * halves * 2
    copies = []

    def store(p, f, level, c, value):
        start = ((p * (fields + 1) + f) * levels + level) * (2 * halves) + c
        rows_ref[pl.ds(start, halves, stride=2), :] = value[:halves]

    def send(p, first, last):
        start, stop = ((p * (fields + 1) + f) * field_rows for f in (first, last))
        out_ref[start:stop] = rows_ref[start:stop, :slots].astype(BF16)
        part = pl.ds(start, stop - start)
        copies.append(pltpu.make_async_copy(out_ref.at[part], out_hbm.at[part], sems.at[len(copies)]))
        copies[-1].start()

    for p in range(2):
        valid = slot_lanes_ref[...] + 2 * half + p <= waves - 1
        for f in range(fields):
            for side in range(2):
                n = (side * fields + f) * 2 + p
                far_n = ((1 - side) * fields + f) * 2 + p
                kept = jnp.concatenate(
                    [total_ref[n, 6:8, :], total_ref[n, 14:16, :], total_ref[n, 22:24, :], jnp.zeros((2, LANES), F32)],
                    axis=0,
                )
                for far, value in enumerate((kept + given(2 - 2 * group, far_n), given(1, far_n) + given(2 * group, far_n))):
                    value = jnp.where(valid, value, 0.0)
                    first = ((y ^ far) * 2 + (core ^ side)) * (levels // 4)
                    for plane in range(planes):
                        l, c = plane // 2, plane % 2
                        shifted = value if plane == 0 else pltpu.roll(value, LANES - plane * width, 1)
                        store(p, f, first + l, c, shifted)
                        if f == fields - 1:
                            temps_ref[first + l, 2 * p + c] = shifted
        send(p, 0, fields)
    for p in range(2):
        for c in range(2):
            temps = [temps_ref[k, 2 * p + c] for k in range(levels)]
            for level in range(levels):
                value = weights_ref[level * levels + level] * temps[level]
                for k in range(level + 1, levels):
                    value += weights_ref[level * levels + k] * temps[k]
                store(p, fields, level, c, value)
        send(p, fields, fields + 1)
    for copy in copies:
        copy.wait()


HBM = pl.BlockSpec(memory_space=pltpu.HBM)
VMEM = pl.BlockSpec(memory_space=pltpu.VMEM)


def fast_body(fourier, legendre, lat_points, wave_slots, vertical):
    fields, local_levels, _, _, _, pairs, waves = fourier.shape
    slots, _, halves, _, sums = legendre.shape
    bands = lax.axis_size("band")
    levels = 4 * local_levels
    planes = 2 * local_levels
    shape = jax.ShapeDtypeStruct

    functions = legendre.transpose(0, 2, 3, 1, 4).reshape(slots * halves * 2, sums)
    other_functions = flipped(functions, "lev", 3)

    rows = fourier.transpose(0, 1, 2, 4, 5, 3, 6).reshape(-1, waves)
    block = shape((2 * fields * pairs, LANES), BF16)
    slot_lanes, functions, vertical, *blocks = pl.pallas_call(
        functools.partial(prepare_kernel, (fields, planes, pairs, slots, waves)),
        in_specs=[HBM] * 5,
        out_specs=[VMEM] * (3 + bands),
        out_shape=[
            shape((8, LANES), jnp.int32),
            shape(functions.shape, BF16),
            shape(vertical.shape, F32),
        ]
        + [block] * bands,
        scratch_shapes=[
            pltpu.SMEM(lat_points.shape, jnp.int32),
            pltpu.SMEM((1, wave_slots.size), jnp.int32),
            pltpu.VMEM(rows.shape, BF16),
            pltpu.SemaphoreType.DMA((4 + PIECES,)),
        ],
        compiler_params=pltpu.CompilerParams(vmem_limit_bytes=GRANT),
        name="prepare",
    )(*[pltpu.with_memory_space_constraint(v, pltpu.HBM) for v in (lat_points, wave_slots.reshape(1, -1), rows, functions, vertical)])

    steps = tuple(range(1, bands))
    own = {0: blocks[0]}
    for k in steps:
        own[k] = lax.ppermute(blocks[k], ("band", "lev"), crossed(k))
    core_functions = flipped(functions, "lev", 1)
    table, weights = pl.pallas_call(
        functools.partial(spread_kernel, (planes, slots, halves, sums)),
        in_specs=[VMEM] * 4,
        out_specs=[VMEM] * 2,
        out_shape=[shape((2, sums * 24, LANES), F32), shape((levels * levels, 8, LANES), F32)],
        scratch_shapes=[pltpu.VMEM((3, slots * halves * 2, LANES), F32)],
        compiler_params=pltpu.CompilerParams(vmem_limit_bytes=GRANT),
        name="spread",
    )(functions, core_functions, other_functions, vertical)
    other = {}
    for k in (0, *steps):
        other[k] = flipped(own[k], "lev", 1)

    count = 4 * fields
    message = shape((count * (halves // 2), LANES), BF16)
    totals = shape((count, 24, LANES), F32)
    parts = [(own[k], (min(k, 1), k)) for k in range(bands)] + [(other[k], (1 - min(k, 1), k)) for k in range(bands)]
    early, others = parts[: bands + 2], parts[bands + 2 :]
    before = pl.pallas_call(
        functools.partial(sum_first_kernel, (fields, pairs, bands), [where for _, where in early]),
        in_specs=[VMEM] * (len(early) + 1),
        out_specs=VMEM,
        out_shape=totals,
        scratch_shapes=[pltpu.VMEM((len(early), *block.shape), F32)],
        compiler_params=pltpu.CompilerParams(vmem_limit_bytes=GRANT),
        name="sum_first",
    )(*[value for value, _ in early], table)
    total, soon, to_y, late = pl.pallas_call(
        functools.partial(sum_kernel, (fields, pairs, bands), [where for _, where in others]),
        in_specs=[VMEM] * (len(others) + 2),
        out_specs=[VMEM] * 4,
        out_shape=[totals] + [message] * 3,
        scratch_shapes=[
            pltpu.VMEM((max(len(others), 1), *block.shape), F32),
            pltpu.VMEM((3, *message.shape), F32),
        ],
        compiler_params=pltpu.CompilerParams(vmem_limit_bytes=GRANT),
        name="sum",
    )(*[value for value, _ in others], table, before)

    levs = lax.axis_size("lev")
    from_soon = lax.ppermute(soon, ("lev", "grp"), round_the_square(levs, 0))
    from_y = flipped(to_y, "lev", 3)
    from_late = lax.ppermute(late, ("lev", "grp"), round_the_square(levs, 1))
    own_halves = halves // 2
    out_rows = 2 * (fields + 1) * levels * own_halves * 2
    out = pl.pallas_call(
        functools.partial(finish_kernel, (fields, levels, own_halves, slots, waves)),
        in_specs=[VMEM] * 6,
        out_specs=HBM,
        out_shape=shape((out_rows, slots), BF16),
        scratch_shapes=[
            pltpu.VMEM((levels, 4, 8, LANES), F32),
            pltpu.VMEM((out_rows + 16, LANES), F32),
            pltpu.VMEM((out_rows, slots), BF16),
            pltpu.VMEM((3, message.shape[0] + 8, LANES), F32),
            pltpu.SemaphoreType.DMA((4,)),
        ],
        compiler_params=pltpu.CompilerParams(vmem_limit_bytes=GRANT),
        name="finish",
    )(weights, slot_lanes, total, from_soon, from_y, from_late)
    out = out.reshape(2, fields + 1, levels, own_halves, 2, slots)
    return out.transpose(5, 0, 1, 2, 4, 3)


def fits(mesh, fourier, legendre):
    bands, levs, groups = (mesh.shape[a] for a in ("band", "lev", "grp"))
    fields, levels, _, _, _, pairs, waves = fourier.shape
    slots, _, halves, _, sums = legendre.shape
    planes = 2 * levels // levs
    return (
        levs == 4
        and groups == 2
        and bands & (bands - 1) == 0
        and waves <= LANES
        and sums <= LANES
        and halves // levs == 12
        and LANES % planes == 0
        and 12 % planes == 0
        and slots // bands <= LANES // planes
        and slots // bands % 8 == 0
        and 2 * pairs // bands % 8 == 0
        and sums % 8 == 0
        and fields * planes * 2 * (pairs // bands) % (16 * PIECES) == 0
    )


def general_body(fourier, legendre, lat_points, wave_slots, vertical):
    wave_count = fourier.shape[6]
    cutoff = jnp.minimum(wave_count - 1, (lat_points - 1) // 2)
    wave_ids = lax.broadcasted_iota(jnp.int32, (1, 1, wave_count), 2)
    kept_mask = wave_ids <= cutoff[:, :, None]
    masked = jnp.where(kept_mask, fourier, jnp.zeros((), fourier.dtype))
    slot_table = (
        wave_slots[:, None] == lax.broadcasted_iota(jnp.int32, (wave_count, wave_count), 1)
    ).astype(jnp.bfloat16)
    ordered = lax.dot_general(
        slot_table, masked, (((1,), (6,)), ((), ())), preferred_element_type=jnp.float32
    ).astype(jnp.bfloat16)
    at_owners = lax.all_to_all(ordered, "band", split_axis=0, concat_axis=6, tiled=True)
    coeffs = lax.all_gather(at_owners, "lev", axis=2, tiled=True)
    level_count = coeffs.shape[2]
    level_rows = lax.broadcasted_iota(jnp.int32, (level_count, level_count), 0)
    level_cols = lax.broadcasted_iota(jnp.int32, (level_count, level_count), 1)
    integral = jnp.where(level_cols >= level_rows, vertical, jnp.zeros((), vertical.dtype))
    geopotential = jnp.einsum(
        "lk,skchgr->slchgr",
        integral,
        coeffs[:, 2].astype(jnp.float32),
        precision=lax.Precision.HIGHEST,
    ).astype(jnp.bfloat16)
    fields = jnp.concatenate([coeffs, geopotential[:, None]], axis=1)
    northern = fields[:, :, :, :, 0].astype(jnp.float32)
    southern = fields[:, :, :, :, 1].astype(jnp.float32)
    parity = jnp.stack(
        [(northern + southern).astype(jnp.bfloat16), (northern - southern).astype(jnp.bfloat16)],
        axis=4,
    )
    partial_value = lax.dot_general(
        parity, legendre, (((5, 6), (3, 4)), ((0, 4), (0, 1))), preferred_element_type=jnp.float32
    )
    groups = lax.axis_size("grp")
    half_count = partial_value.shape[5] // groups
    me = lax.axis_index("grp")
    summed = lax.dynamic_slice_in_dim(partial_value, me * half_count, half_count, 5)
    for step in range(1, groups):
        target = lax.rem(me + step, groups)
        piece = lax.dynamic_slice_in_dim(partial_value, target * half_count, half_count, 5)
        summed = summed + lax.ppermute(
            piece, "grp", [(i, (i + step) % groups) for i in range(groups)]
        )
    slot_count = summed.shape[0]
    slot_waves = lax.dynamic_slice_in_dim(
        wave_slots, lax.axis_index("band") * slot_count, slot_count
    )
    block_start = (lax.axis_index("lev") * groups + me) * half_count
    half_ids = block_start + lax.broadcasted_iota(jnp.int32, (1, 1, half_count), 2)
    parity_ids = lax.broadcasted_iota(jnp.int32, (1, 2, 1), 1)
    total = slot_waves[:, None, None] + 2 * half_ids + parity_ids
    valid = (total <= wave_count - 1)[:, :, None, None, None, :]
    return jnp.where(valid, summed, 0.0).astype(jnp.bfloat16)


def solution(mesh):
    def program(fourier, legendre, lat_points, wave_slots, vertical):
        placed = (
            P(None, "lev", None, None, "grp", "band", None),
            P("band", None, "lev", "grp", None),
            P("grp", "band"),
            P(),
            P(),
        )
        fast = fits(mesh, fourier, legendre)
        step = jax.shard_map(
            fast_body if fast else general_body,
            mesh=mesh,
            in_specs=placed,
            out_specs=P("band", None, None, None, None, ("lev", "grp")),
            check_vma=False,
        )
        return step(fourier, legendre, lat_points, wave_slots, vertical)

    return program
```
